32 devices in a mesh: dp: 32 (over z, y, x, core).
Axes of the slice: x: 2, y: 2, z: 4, core: 2. Of those that a mesh axis runs over, the one named last changes fastest.
Arguments:
- inputs: float32 [6144, 576], P('dp'), may hold values from -6 to 6
- cotangent: float32 [6144, 576], P('dp'), may hold values from -6 to 6
- attn_shard: bfloat16 [884736], P('dp'), may hold values from -10 to 10
- mlp_shard: bfloat16 [2654208], P('dp'), may hold values from -0.25 to 0.25
- gain_rows: float32 [2, 576], replicated, may hold values from 0.5 to 1.5
Outputs:
- outputs: float32 [6144, 576], P('dp')
- input_grad: float32 [6144, 576], P('dp')
- attn_grad: float32 [884736], P('dp')
- mlp_grad: float32 [2654208], P('dp')
- gain_grad: float32 [2, 576], replicated
The draws below stay inside these ranges and needn't reach their ends.
All inputs are finite; a program needn't handle non-finite values.
Results may differ from the reference program's by a relative error of at most 0.014.
Values may be sent and summed in bfloat16 or wider, within the bound.
A program may use at most 128 MiB of HBM per device.

```python
import math
import jax
import jax.numpy as jnp
from jax import lax

D = 576
HEADS = 9
KV_HEADS = 3
HEAD_DIM = 64
FF = 1536
SEQ_LEN = 192
TOKENS = 6144
MLP_P = 2654208


def draw_attn_shard(key, part):
    kv_width = KV_HEADS * HEAD_DIM
    sub_keys = jax.random.split(jax.random.fold_in(key, 11), 4)
    w_query = jax.random.truncated_normal(sub_keys[0], -4.0, 4.0, (D, D), jnp.float32) * D ** (-0.5)
    w_key = jax.random.truncated_normal(sub_keys[1], -4.0, 4.0, (D, kv_width), jnp.float32) * D ** (-0.5)
    w_value = jax.random.truncated_normal(sub_keys[2], -4.0, 4.0, (D, kv_width), jnp.float32) * D ** (-0.5)
    w_out = jax.random.truncated_normal(sub_keys[3], -4.0, 4.0, (D, D), jnp.float32) * 3.0 * D ** (-0.5)
    return jnp.concatenate([w_query.ravel(), w_key.ravel(), w_value.ravel(), w_out.ravel()]).astype(jnp.bfloat16)


def steps_of(stream_key, dims, cuts, least, largest):
    factor_of = 1.0
    for dim, blocks in cuts:
        draws = jax.random.uniform(jax.random.fold_in(jax.random.fold_in(stream_key, 6), dim), (blocks,), jnp.float32, least / len(cuts), largest / len(cuts))
        factor_of = factor_of * jnp.repeat(jnp.exp(draws), dims[dim] // blocks).reshape((-1,) + (1,) * (len(dims) - 1 - dim))
    return factor_of


def normal_values(key, extent, scale, most, cuts=(), kind=jnp.bfloat16):
    drawn = jax.random.normal(key, extent, jnp.float32) * scale
    if len(cuts) > 0:
        drawn = steps_of(key, extent, cuts, -0.22, 0.18) * drawn
    return jnp.clip(drawn, min=-most, max=most).astype(kind)


def setup_inputs(seed: int = 0) -> dict:
    splits = jax.random.split(jax.random.key(seed), 6)
    return {
        "inputs": normal_values(splits[0], (TOKENS, D), 1.0, 6.0, ((0, 32),), jnp.float32),
        "cotangent": normal_values(splits[1], (TOKENS, D), 1.0, 6.0, ((0, 32),), jnp.float32),
        "attn_shard": draw_attn_shard(jax.random.fold_in(splits[5], 71), 0),
        "mlp_shard": normal_values(splits[3], (MLP_P,), D ** -0.5, 0.25, ((0, 32),)),
        "gain_rows": jnp.clip(1.0 + 0.1 * jax.random.normal(splits[4], (2, D), jnp.float32), 0.5, 1.5),
    }


EPS = 1e-05
THETA = 100000.0

def mix(form, left, right):
    return jnp.einsum(form, left.astype(jnp.float32), right.astype(jnp.float32))

def matmul(left, right):
    return jnp.dot(left, right, preferred_element_type=jnp.float32)

def inner(left, right):
    return lax.dot_general(left, right, (((0,), (0,)), ((), ())), preferred_element_type=jnp.float32)

def outer_t(left, right):
    return lax.dot_general(left, right, (((1,), (1,)), ((), ())), preferred_element_type=jnp.float32)

def split_attention(flat):
    kv_width = KV_HEADS * HEAD_DIM
    edge_one = D * D
    edge_two = edge_one + D * kv_width
    edge_three = edge_two + D * kv_width
    return (flat[:edge_one].reshape(D, D), flat[edge_one:edge_two].reshape(D, kv_width), flat[edge_two:edge_three].reshape(D, kv_width), flat[edge_three:].reshape(D, D))

def split_mlp(flat):
    edge_one = D * FF
    return (flat[:edge_one].reshape(D, FF), flat[edge_one:2 * edge_one].reshape(D, FF), flat[2 * edge_one:].reshape(FF, D))

def rope_tables():
    position = jnp.arange(SEQ_LEN).astype(jnp.float32)
    frequency = THETA ** (-(jnp.arange(HEAD_DIM // 2).astype(jnp.float32) * 2.0 / HEAD_DIM))
    angles = position[:, None] * frequency[None, :]
    return (jnp.cos(angles), jnp.sin(angles))

def rotate(tensor, cosine, sine_tab):
    half_dim = tensor.shape[-1] // 2
    lower_half = tensor[..., :half_dim]
    upper_half = tensor[..., half_dim:]
    cos_wide = cosine[None, :, None, :]
    sin_wide = sine_tab[None, :, None, :]
    return jnp.concatenate([lower_half * cos_wide - upper_half * sin_wide, upper_half * cos_wide + lower_half * sin_wide], axis=-1)

def norm_forward(stream, gain_row):
    inv_rms = lax.rsqrt(lax.optimization_barrier(jnp.mean(stream * stream, axis=-1, keepdims=True)) + EPS)
    normed = stream * inv_rms
    return (normed, inv_rms, (normed * gain_row).astype(jnp.bfloat16))

def norm_backward(grad_in, normed, inv_rms, gain_row):
    scaled = grad_in * gain_row
    grad_stream = inv_rms * (scaled - normed * lax.optimization_barrier(jnp.mean(scaled * normed, axis=-1, keepdims=True)))
    return (grad_stream, lax.optimization_barrier(jnp.sum(grad_in * normed, axis=0)))

def scores_of(queries, key_rot):
    raw_scores = mix('sqkgd,stkd->skgqt', queries, key_rot) * HEAD_DIM ** (-0.5)
    causal = jnp.arange(SEQ_LEN)[:, None] >= jnp.arange(SEQ_LEN)[None, :]
    return jnp.where(causal, raw_scores, -jnp.inf)

def forward(stream, attn_weights, mlp_weights, gain_rows):
    w_query, w_key, w_value, w_out = attn_weights
    w_gate, w_up, w_down = mlp_weights
    row_count = stream.shape[0]
    seq_count = row_count // SEQ_LEN
    group_size = HEADS // KV_HEADS
    cosine, sine_tab = rope_tables()
    normed_one, inv_one, entry_one = norm_forward(stream, gain_rows[0])
    queries = matmul(entry_one, w_query).reshape(seq_count, SEQ_LEN, HEADS, HEAD_DIM)
    queries = rotate(queries, cosine, sine_tab).astype(jnp.bfloat16).reshape(seq_count, SEQ_LEN, KV_HEADS, group_size, HEAD_DIM)
    key_rot = rotate(matmul(entry_one, w_key).reshape(seq_count, SEQ_LEN, KV_HEADS, HEAD_DIM), cosine, sine_tab).astype(jnp.bfloat16)
    values = matmul(entry_one, w_value).astype(jnp.bfloat16).reshape(seq_count, SEQ_LEN, KV_HEADS, HEAD_DIM)
    scores = scores_of(queries, key_rot)
    row_top = lax.optimization_barrier(jnp.max(scores, axis=-1, keepdims=True))
    log_total = row_top + jnp.log(lax.optimization_barrier(jnp.sum(jnp.exp(scores - row_top), axis=-1, keepdims=True)))
    attn_probs = jnp.exp(scores - log_total).astype(jnp.bfloat16)
    context = mix('skgqt,stkd->sqkgd', attn_probs, values).astype(jnp.bfloat16).reshape(row_count, D)
    middle = stream + matmul(context, w_out)
    normed_two, inv_two, entry_two = norm_forward(middle, gain_rows[1])
    gate_pre = matmul(entry_two, w_gate)
    upward = matmul(entry_two, w_up)
    hidden = (jax.nn.silu(gate_pre) * upward).astype(jnp.bfloat16)
    output = middle + matmul(hidden, w_down)
    kept_state = (normed_one, inv_one, entry_one, queries, key_rot, values, log_total, context, normed_two, inv_two, entry_two, gate_pre, upward, hidden)
    return (output, kept_state)

def mlp_backward(grad_out, kept_state, mlp_weights, gain_rows):
    normed_two, inv_two, entry_two, gate_pre, upward, hidden = kept_state[8:]
    w_gate, w_up, w_down = mlp_weights
    grad_bf = grad_out.astype(jnp.bfloat16)
    grad_down = inner(hidden, grad_bf)
    grad_hidden = outer_t(grad_bf, w_down)
    sigma = jax.nn.sigmoid(gate_pre)
    grad_gate = (grad_hidden * upward * sigma * (1.0 + gate_pre * (1.0 - sigma))).astype(jnp.bfloat16)
    grad_upward = (grad_hidden * gate_pre * sigma).astype(jnp.bfloat16)
    grad_gate_w = inner(entry_two, grad_gate)
    grad_up_w = inner(entry_two, grad_upward)
    grad_entry = outer_t(grad_gate, w_gate) + outer_t(grad_upward, w_up)
    grad_norm, gain_two = norm_backward(grad_entry, normed_two, inv_two, gain_rows[1])
    flat_grad = jnp.concatenate([grad_gate_w.ravel(), grad_up_w.ravel(), grad_down.ravel()])
    return (grad_out + grad_norm, flat_grad, gain_two)

def attn_backward(grad_middle, kept_state, attn_weights, gain_rows):
    normed_one, inv_one, entry_one, queries, key_rot, values, log_total, context = kept_state[:8]
    w_query, w_key, w_value, w_out = attn_weights
    row_count = grad_middle.shape[0]
    seq_count = row_count // SEQ_LEN
    group_size = HEADS // KV_HEADS
    kv_width = KV_HEADS * HEAD_DIM
    cosine, sine_tab = rope_tables()
    grad_bf = grad_middle.astype(jnp.bfloat16)
    grad_out_w = inner(context, grad_bf)
    grad_context = outer_t(grad_bf, w_out).astype(jnp.bfloat16).reshape(seq_count, SEQ_LEN, KV_HEADS, group_size, HEAD_DIM)
    soft_probs = jnp.exp(scores_of(queries, key_rot) - log_total)
    grad_soft = mix('sqkgd,stkd->skgqt', grad_context, values)
    row_dot = lax.optimization_barrier(jnp.sum(soft_probs * grad_soft, axis=-1, keepdims=True))
    grad_scores = (soft_probs * (grad_soft - row_dot) * HEAD_DIM ** (-0.5)).astype(jnp.bfloat16)
    grad_query = mix('skgqt,stkd->sqkgd', grad_scores, key_rot).reshape(seq_count, SEQ_LEN, HEADS, HEAD_DIM)
    grad_query = rotate(grad_query, cosine, -sine_tab).astype(jnp.bfloat16).reshape(row_count, D)
    grad_key = rotate(mix('skgqt,sqkgd->stkd', grad_scores, queries), cosine, -sine_tab).astype(jnp.bfloat16).reshape(row_count, kv_width)
    grad_value = mix('skgqt,sqkgd->stkd', soft_probs.astype(jnp.bfloat16), grad_context).astype(jnp.bfloat16).reshape(row_count, kv_width)
    grad_entry = outer_t(grad_query, w_query) + outer_t(grad_key, w_key) + outer_t(grad_value, w_value)
    grad_norm, gain_one = norm_backward(grad_entry, normed_one, inv_one, gain_rows[0])
    flat_grad = jnp.concatenate([inner(entry_one, grad_query).ravel(), inner(entry_one, grad_key).ravel(), inner(entry_one, grad_value).ravel(), grad_out_w.ravel()])
    return (grad_middle + grad_norm, flat_grad, gain_one)

def reference(inputs, cotangent, attn_shard, mlp_shard, gain_rows):
    attn_weights = split_attention(attn_shard)
    mlp_weights = split_mlp(mlp_shard)
    seq_total = inputs.shape[0] // SEQ_LEN
    block_rows = math.gcd(seq_total, 16) * SEQ_LEN
    blocks_in = inputs.reshape(-1, block_rows, D)
    blocks_cot = cotangent.reshape(-1, block_rows, D)

    def one_block(carry, pieces):
        attn_sum, mlp_sum, gain_sum = carry
        block_in, block_cot = pieces
        output, kept_state = forward(block_in, attn_weights, mlp_weights, gain_rows)
        grad_middle, mlp_flat, gain_two = mlp_backward(block_cot, kept_state, mlp_weights, gain_rows)
        grad_input, attn_flat, gain_one = attn_backward(grad_middle, kept_state, attn_weights, gain_rows)
        carry_next = (attn_sum + attn_flat, mlp_sum + mlp_flat, gain_sum + jnp.stack([gain_one, gain_two]))
        return (carry_next, (output, grad_input))
    start_carry = (jnp.zeros(attn_shard.shape, jnp.float32), jnp.zeros(mlp_shard.shape, jnp.float32), jnp.zeros((2, D), jnp.float32))
    totals, results = lax.scan(one_block, start_carry, (blocks_in, blocks_cot))
    attn_grad, mlp_grad, gain_grad = totals
    outputs, input_grad = results
    return (outputs.reshape(-1, D), input_grad.reshape(-1, D), attn_grad, mlp_grad, gain_grad)
```

```python
import jax
import jax.numpy as jnp
from jax import lax
from jax.experimental import pallas as pl
from jax.experimental.pallas import tpu as pltpu
from jax.sharding import PartitionSpec as P

LANES = 128
PIECES = 6
MESH = pl.DeviceIdType.MESH

D = 576
HEADS = 9
KV_HEADS = 3
HEAD_DIM = 64
FF = 1536
SEQ_LEN = 192


EPS = 1e-05
THETA = 100000.0


def mix(form, left, right):
    return jnp.einsum(form, left, right, preferred_element_type=jnp.float32)


def matmul(left, right):
    return jnp.dot(left, right, preferred_element_type=jnp.float32)


def inner(left, right):
    return lax.dot_general(
        left, right, (((0,), (0,)), ((), ())), preferred_element_type=jnp.float32
    )


def outer_t(left, right):
    return lax.dot_general(
        left, right, (((1,), (1,)), ((), ())), preferred_element_type=jnp.float32
    )


def split_attention(flat):
    kv_width = KV_HEADS * HEAD_DIM
    edge_one = D * D
    edge_two = edge_one + D * kv_width
    edge_three = edge_two + D * kv_width
    return (
        flat[:edge_one].reshape(D, D),
        flat[edge_one:edge_two].reshape(D, kv_width),
        flat[edge_two:edge_three].reshape(D, kv_width),
        flat[edge_three:].reshape(D, D),
    )


def split_mlp(flat):
    edge_one = D * FF
    return (
        flat[:edge_one].reshape(D, FF),
        flat[edge_one : 2 * edge_one].reshape(D, FF),
        flat[2 * edge_one :].reshape(FF, D),
    )


def rope_tables():
    position = jnp.arange(SEQ_LEN).astype(jnp.float32)
    frequency = THETA ** (-(jnp.arange(HEAD_DIM // 2).astype(jnp.float32) * 2.0 / HEAD_DIM))
    angles = position[:, None] * frequency[None, :]
    return (jnp.cos(angles), jnp.sin(angles))


def rotate(tensor, cosine, sine_tab):
    half_dim = tensor.shape[-1] // 2
    lower_half = tensor[..., :half_dim]
    upper_half = tensor[..., half_dim:]
    cos_wide = cosine[None, :, None, :]
    sin_wide = sine_tab[None, :, None, :]
    return jnp.concatenate(
        [
            lower_half * cos_wide - upper_half * sin_wide,
            upper_half * cos_wide + lower_half * sin_wide,
        ],
        axis=-1,
    )


def norm_forward(stream, gain_row):
    inv_rms = lax.rsqrt(jnp.mean(stream * stream, axis=-1, keepdims=True) + EPS)
    normed = stream * inv_rms
    return (normed, inv_rms, (normed * gain_row).astype(jnp.bfloat16))


def norm_backward(grad_in, normed, inv_rms, gain_row):
    scaled = grad_in * gain_row
    grad_stream = inv_rms * (scaled - normed * jnp.mean(scaled * normed, axis=-1, keepdims=True))
    return (grad_stream, jnp.sum(grad_in * normed, axis=0))


def scores_of(queries, key_rot):
    raw_scores = mix("sqkgd,stkd->skgqt", queries, key_rot) * HEAD_DIM ** (-0.5)
    causal = jnp.arange(SEQ_LEN)[:, None] >= jnp.arange(SEQ_LEN)[None, :]
    return jnp.where(causal, raw_scores, -jnp.inf)


def forward(stream, attn_weights, mlp_weights, gain_rows):
    w_query, w_key, w_value, w_out = attn_weights
    w_gate, w_up, w_down = mlp_weights
    row_count = stream.shape[0]
    seq_count = row_count // SEQ_LEN
    group_size = HEADS // KV_HEADS
    cosine, sine_tab = rope_tables()
    normed_one, inv_one, entry_one = norm_forward(stream, gain_rows[0])
    queries = matmul(entry_one, w_query).reshape(seq_count, SEQ_LEN, HEADS, HEAD_DIM)
    queries = (
        rotate(queries, cosine, sine_tab)
        .astype(jnp.bfloat16)
        .reshape(seq_count, SEQ_LEN, KV_HEADS, group_size, HEAD_DIM)
    )
    key_rot = rotate(
        matmul(entry_one, w_key).reshape(seq_count, SEQ_LEN, KV_HEADS, HEAD_DIM), cosine, sine_tab
    ).astype(jnp.bfloat16)
    values = (
        matmul(entry_one, w_value)
        .astype(jnp.bfloat16)
        .reshape(seq_count, SEQ_LEN, KV_HEADS, HEAD_DIM)
    )
    scores = scores_of(queries, key_rot)
    row_top = jnp.max(scores, axis=-1, keepdims=True)
    log_total = row_top + jnp.log(jnp.sum(jnp.exp(scores - row_top), axis=-1, keepdims=True))
    attn_probs = jnp.exp(scores - log_total).astype(jnp.bfloat16)
    context = (
        mix("skgqt,stkd->sqkgd", attn_probs, values).astype(jnp.bfloat16).reshape(row_count, D)
    )
    middle = stream + matmul(context, w_out)
    normed_two, inv_two, entry_two = norm_forward(middle, gain_rows[1])
    gate_pre = matmul(entry_two, w_gate)
    upward = matmul(entry_two, w_up)
    hidden = (jax.nn.silu(gate_pre) * upward).astype(jnp.bfloat16)
    output = middle + matmul(hidden, w_down)
    kept_state = (
        normed_one,
        inv_one,
        entry_one,
        queries,
        key_rot,
        values,
        log_total,
        context,
        normed_two,
        inv_two,
        entry_two,
        gate_pre,
        upward,
        hidden,
    )
    return (output, kept_state)


def flatten(grads):
    return jnp.concatenate([grad.astype(jnp.bfloat16).ravel() for grad in grads])


def mlp_backward(grad_out, kept_state, mlp_weights, gain_rows):
    normed_two, inv_two, entry_two, gate_pre, upward, hidden = kept_state[8:]
    w_gate, w_up, w_down = mlp_weights
    grad_bf = grad_out.astype(jnp.bfloat16)
    grad_down = inner(hidden, grad_bf)
    grad_hidden = outer_t(grad_bf, w_down)
    sigma = jax.nn.sigmoid(gate_pre)
    grad_gate = (grad_hidden * upward * sigma * (1.0 + gate_pre * (1.0 - sigma))).astype(
        jnp.bfloat16
    )
    grad_upward = (grad_hidden * gate_pre * sigma).astype(jnp.bfloat16)
    grad_gate_w = inner(entry_two, grad_gate)
    grad_up_w = inner(entry_two, grad_upward)
    grad_entry = outer_t(grad_gate, w_gate) + outer_t(grad_upward, w_up)
    grad_norm, gain_two = norm_backward(grad_entry, normed_two, inv_two, gain_rows[1])
    flat_grad = flatten([grad_gate_w, grad_up_w, grad_down])
    return (grad_out + grad_norm, flat_grad, gain_two)


def attn_backward(grad_middle, kept_state, attn_weights, gain_rows):
    normed_one, inv_one, entry_one, queries, key_rot, values, log_total, context = kept_state[:8]
    w_query, w_key, w_value, w_out = attn_weights
    row_count = grad_middle.shape[0]
    seq_count = row_count // SEQ_LEN
    group_size = HEADS // KV_HEADS
    kv_width = KV_HEADS * HEAD_DIM
    cosine, sine_tab = rope_tables()
    grad_bf = grad_middle.astype(jnp.bfloat16)
    grad_out_w = inner(context, grad_bf)
    grad_context = (
        outer_t(grad_bf, w_out)
        .astype(jnp.bfloat16)
        .reshape(seq_count, SEQ_LEN, KV_HEADS, group_size, HEAD_DIM)
    )
    soft_probs = jnp.exp(scores_of(queries, key_rot) - log_total)
    grad_soft = mix("sqkgd,stkd->skgqt", grad_context, values)
    row_dot = jnp.sum(soft_probs * grad_soft, axis=-1, keepdims=True)
    grad_scores = (soft_probs * (grad_soft - row_dot) * HEAD_DIM ** (-0.5)).astype(jnp.bfloat16)
    grad_query = mix("skgqt,stkd->sqkgd", grad_scores, key_rot).reshape(
        seq_count, SEQ_LEN, HEADS, HEAD_DIM
    )
    grad_query = rotate(grad_query, cosine, -sine_tab).astype(jnp.bfloat16).reshape(row_count, D)
    grad_key = (
        rotate(mix("skgqt,sqkgd->stkd", grad_scores, queries), cosine, -sine_tab)
        .astype(jnp.bfloat16)
        .reshape(row_count, kv_width)
    )
    grad_value = (
        mix("skgqt,sqkgd->stkd", soft_probs.astype(jnp.bfloat16), grad_context)
        .astype(jnp.bfloat16)
        .reshape(row_count, kv_width)
    )
    grad_entry = (
        outer_t(grad_query, w_query) + outer_t(grad_key, w_key) + outer_t(grad_value, w_value)
    )
    grad_norm, gain_one = norm_backward(grad_entry, normed_one, inv_one, gain_rows[0])
    flat_grad = flatten(
        [
            inner(entry_one, grad_query),
            inner(entry_one, grad_key),
            inner(entry_one, grad_value),
            grad_out_w,
        ]
    )
    return (grad_middle + grad_norm, flat_grad, gain_one)


def bit_count(devices):
    bits = devices.bit_length() - 1
    assert 1 << bits == devices
    return bits


def bit_orders(bits):
    plain = list(range(bits - 1, -1, -1))
    swapped = list(plain)
    if bits > 2:
        first, second = swapped.index(2), swapped.index(1)
        swapped[first], swapped[second] = swapped[second], swapped[first]
    return [plain if piece % 2 == 0 else swapped for piece in range(PIECES)]


def coordinates(bits):
    me = lax.axis_index("dp")
    digits = [lax.rem(me // (1 << bit), 2) for bit in range(bits)]
    partners = [me + (1 << bit) * (1 - 2 * digits[bit]) for bit in range(bits)]
    return digits, partners


def meet(partners):
    barrier = pltpu.get_barrier_semaphore()
    for partner in partners:
        pl.semaphore_signal(barrier, inc=1, device_id=(partner,), device_id_type=MESH)
    pl.semaphore_wait(barrier, len(partners))


def pick(bits, fixed):
    return tuple(fixed.get(bit, slice(None)) for bit in range(bits - 1, -1, -1))


def gather_kernel(bits, shard_ref, full_ref, local_sem, send_sem, recv_sem):
    digits, partners = coordinates(bits)
    orders = bit_orders(bits)
    own = pltpu.make_async_copy(
        shard_ref, full_ref.at[pick(bits, dict(enumerate(digits)))], local_sem
    )
    own.start()
    meet(partners)
    own.wait()
    flights = {}
    for stage in range(bits):
        for piece in range(PIECES):
            if stage > 0:
                flights[piece, stage - 1].wait_recv()
            order = orders[piece]
            fixed = {bit: digits[bit] for bit in order[stage:]}
            block = full_ref.at[pick(bits, fixed) + (piece,)]
            copy = pltpu.make_async_remote_copy(
                src_ref=block,
                dst_ref=block,
                send_sem=send_sem.at[piece, stage],
                recv_sem=recv_sem.at[piece, stage],
                device_id=(partners[order[stage]],),
                device_id_type=MESH,
            )
            copy.start()
            flights[piece, stage] = copy
    for piece in range(PIECES):
        flights[piece, bits - 1].wait_recv()
    for copy in flights.values():
        copy.wait_send()


def gather(shard):
    devices = lax.axis_size("dp")
    bits = bit_count(devices)
    rows = shard.shape[0] // PIECES
    full = pl.pallas_call(
        lambda *refs: gather_kernel(bits, *refs),
        out_shape=jax.ShapeDtypeStruct((2,) * bits + (PIECES, rows, LANES), shard.dtype),
        in_specs=[pl.BlockSpec(memory_space=pltpu.VMEM)],
        out_specs=pl.BlockSpec(memory_space=pltpu.VMEM),
        scratch_shapes=[
            pltpu.SemaphoreType.DMA,
            pltpu.SemaphoreType.DMA((PIECES, bits)),
            pltpu.SemaphoreType.DMA((PIECES, bits)),
        ],
        compiler_params=pltpu.CompilerParams(
            collective_id=0, has_side_effects=True, vmem_limit_bytes=60 << 20
        ),
    )(shard.reshape(PIECES, rows, LANES))
    return full.reshape(devices, PIECES * rows, LANES)


def scatter_kernel(bits, total_ref, gain_ref, out_ref, gain_out, *scratch):
    landing = scratch[:bits]
    held = scratch[bits : 2 * bits - 1]
    gain_sent, gain_landing = scratch[2 * bits - 1 : 2 * bits + 1]
    send_sem, recv_sem, gain_send, gain_recv = scratch[2 * bits + 1 :]
    digits, partners = coordinates(bits)
    orders = [order[::-1] for order in bit_orders(bits)]
    meet(partners)
    flights = {}
    gain_flights = {}

    def block_index(order, stage, digit):
        if stage == 0:
            return pick(bits, {order[0]: digit})
        left = [bit for bit in range(bits - 1, -1, -1) if bit not in order[:stage]]
        return tuple(digit if bit == order[stage] else slice(None) for bit in left)

    def source(piece, stage):
        return total_ref if stage == 0 else held[stage - 1]

    def launch(piece, stage):
        order = orders[piece]
        bit = order[stage]
        lead = block_index(order, stage, 1 - digits[bit])
        if stage == 0:
            src = total_ref.at[lead + (piece,)]
        else:
            src = held[stage - 1].at[(piece,) + lead]
        copy = pltpu.make_async_remote_copy(
            src_ref=src,
            dst_ref=landing[stage].at[piece],
            send_sem=send_sem.at[piece, stage],
            recv_sem=recv_sem.at[piece, stage],
            device_id=(partners[bit],),
            device_id_type=MESH,
        )
        copy.start()
        flights[piece, stage] = copy

    def absorb(piece, stage):
        flights[piece, stage].wait_recv()
        order = orders[piece]
        bit = order[stage]
        lead = block_index(order, stage, digits[bit])
        free = len(lead) - 1
        for number in range(1 << free):
            picks = [(number >> place) & 1 for place in range(free - 1, -1, -1)]
            spot = iter(picks)
            where = tuple(next(spot) if isinstance(item, slice) else item for item in lead)
            if stage == 0:
                mine = total_ref[where + (piece,)]
            else:
                mine = held[stage - 1][(piece,) + where]
            other = landing[stage][(piece,) + tuple(picks)]
            value = mine.astype(jnp.float32) + other.astype(jnp.float32)
            if stage == bits - 1:
                out_ref[piece] = value
            else:
                held[stage][(piece,) + tuple(picks)] = value.astype(jnp.bfloat16)

    def launch_gain(stage):
        copy = pltpu.make_async_remote_copy(
            src_ref=gain_ref if stage == 0 else gain_sent.at[stage],
            dst_ref=gain_landing.at[stage],
            send_sem=gain_send.at[stage],
            recv_sem=gain_recv.at[stage],
            device_id=(partners[stage],),
            device_id_type=MESH,
        )
        copy.start()
        gain_flights[stage] = copy

    def absorb_gain(stage):
        gain_flights[stage].wait_recv()
        mine = gain_ref[...] if stage == 0 else gain_sent[stage]
        value = mine + gain_landing[stage]
        if stage == bits - 1:
            gain_out[...] = value
        else:
            gain_sent[stage + 1] = value

    for stage in range(bits):
        if stage > 0:
            absorb_gain(stage - 1)
        launch_gain(stage)
        for piece in range(PIECES):
            if stage > 0:
                absorb(piece, stage - 1)
            launch(piece, stage)
    absorb_gain(bits - 1)
    for piece in range(PIECES):
        absorb(piece, bits - 1)
    for copy in list(flights.values()) + list(gain_flights.values()):
        copy.wait_send()


def scatter(total, gains):
    devices = lax.axis_size("dp")
    bits = bit_count(devices)
    rows = total.shape[1] // PIECES
    slots = [(PIECES,) + (2,) * (bits - 1 - stage) + (rows, LANES) for stage in range(bits)]
    vmem = pl.BlockSpec(memory_space=pltpu.VMEM)
    out, gain_sum = pl.pallas_call(
        lambda *refs: scatter_kernel(bits, *refs),
        out_shape=(
            jax.ShapeDtypeStruct((PIECES, rows, LANES), jnp.float32),
            jax.ShapeDtypeStruct(gains.shape, jnp.float32),
        ),
        in_specs=[vmem, vmem],
        out_specs=(vmem, vmem),
        scratch_shapes=[pltpu.VMEM(slot, jnp.bfloat16) for slot in slots]
        + [pltpu.VMEM(slot, jnp.bfloat16) for slot in slots[:-1]]
        + [
            pltpu.VMEM((bits,) + gains.shape, jnp.float32),
            pltpu.VMEM((bits,) + gains.shape, jnp.float32),
            pltpu.SemaphoreType.DMA((PIECES, bits)),
            pltpu.SemaphoreType.DMA((PIECES, bits)),
            pltpu.SemaphoreType.DMA((bits,)),
            pltpu.SemaphoreType.DMA((bits,)),
        ],
        compiler_params=pltpu.CompilerParams(
            collective_id=1, has_side_effects=True, vmem_limit_bytes=60 << 20
        ),
    )(total.reshape((2,) * bits + (PIECES, rows, LANES)), gains)
    return out.reshape(PIECES * rows, LANES), gain_sum


def body(inputs, cotangent, attn_shard, mlp_shard, gain_rows):
    devices = lax.axis_size("dp")
    attn_rows = attn_shard.shape[0] // LANES
    packed = jnp.concatenate(
        [attn_shard.reshape(-1, LANES), mlp_shard.reshape(-1, LANES)], axis=0
    )
    full = gather(packed)
    attn_weights = split_attention(full[:, :attn_rows].reshape(-1))
    mlp_weights = split_mlp(full[:, attn_rows:].reshape(-1))
    outputs, kept_state = forward(inputs, attn_weights, mlp_weights, gain_rows)
    grad_middle, mlp_flat, gain_two = mlp_backward(cotangent, kept_state, mlp_weights, gain_rows)
    grad_input, attn_flat, gain_one = attn_backward(
        grad_middle, kept_state, attn_weights, gain_rows
    )
    total = jnp.concatenate(
        [
            attn_flat.reshape(devices, -1, LANES),
            mlp_flat.reshape(devices, -1, LANES),
        ],
        axis=1,
    )
    gains = jnp.stack([gain_one, gain_two])
    summed, gain_grad = scatter(total, gains)
    attn_grad = summed[:attn_rows].reshape(-1)
    mlp_grad = summed[attn_rows:].reshape(-1)
    return (outputs, grad_input, attn_grad, mlp_grad, gain_grad)


def solution(mesh):
    placed = (P("dp", None), P("dp", None), P("dp"), P("dp"), P())
    return jax.shard_map(
        body,
        mesh=mesh,
        in_specs=placed,
        out_specs=(P("dp", None), P("dp", None), P("dp"), P("dp"), P()),
        check_vma=False,
    )
```

```python
import jax
import jax.numpy as jnp
from jax import lax
from jax.experimental import pallas as pl
from jax.experimental.pallas import tpu as pltpu
from jax.sharding import PartitionSpec as P

LANES = 128
ATTN_PIECES = 3
MLP_PIECES = 9
PIECES = ATTN_PIECES + MLP_PIECES
CHUNK = 96
WIDEN = 288
MESH = pl.DeviceIdType.MESH

D = 576
HEADS = 9
KV_HEADS = 3
HEAD_DIM = 64
FF = 1536
SEQ_LEN = 192


EPS = 1e-05
THETA = 100000.0


def mix(form, left, right):
    return jnp.einsum(form, left, right, preferred_element_type=jnp.float32)


def matmul(left, right):
    return jnp.dot(left, right, preferred_element_type=jnp.float32)


def inner(left, right):
    return lax.dot_general(
        left, right, (((0,), (0,)), ((), ())), preferred_element_type=jnp.float32
    )


def outer_t(left, right):
    return lax.dot_general(
        left, right, (((1,), (1,)), ((), ())), preferred_element_type=jnp.float32
    )


def split_attention(flat):
    kv_width = KV_HEADS * HEAD_DIM
    edge_one = D * D
    edge_two = edge_one + D * kv_width
    edge_three = edge_two + D * kv_width
    return (
        flat[:edge_one].reshape(D, D),
        flat[edge_one:edge_two].reshape(D, kv_width),
        flat[edge_two:edge_three].reshape(D, kv_width),
        flat[edge_three:].reshape(D, D),
    )


def split_mlp(flat):
    edge_one = D * FF
    return (
        flat[:edge_one].reshape(D, FF),
        flat[edge_one : 2 * edge_one].reshape(D, FF),
        flat[2 * edge_one :].reshape(FF, D),
    )


def rope_tables():
    position = jnp.arange(SEQ_LEN).astype(jnp.float32)
    frequency = THETA ** (-(jnp.arange(HEAD_DIM // 2).astype(jnp.float32) * 2.0 / HEAD_DIM))
    angles = position[:, None] * frequency[None, :]
    return (jnp.cos(angles), jnp.sin(angles))


def rotate(tensor, cosine, sine_tab):
    half_dim = tensor.shape[-1] // 2
    lower_half = tensor[..., :half_dim]
    upper_half = tensor[..., half_dim:]
    cos_wide = cosine[None, :, None, :]
    sin_wide = sine_tab[None, :, None, :]
    return jnp.concatenate(
        [
            lower_half * cos_wide - upper_half * sin_wide,
            upper_half * cos_wide + lower_half * sin_wide,
        ],
        axis=-1,
    )


def norm_forward(stream, gain_row):
    inv_rms = lax.rsqrt(jnp.mean(stream * stream, axis=-1, keepdims=True) + EPS)
    normed = stream * inv_rms
    return (normed, inv_rms, (normed * gain_row).astype(jnp.bfloat16))


def norm_backward(grad_in, normed, inv_rms, gain_row):
    scaled = grad_in * gain_row
    grad_stream = inv_rms * (scaled - normed * jnp.mean(scaled * normed, axis=-1, keepdims=True))
    return (grad_stream, jnp.sum(grad_in * normed, axis=0))


def scores_of(queries, key_rot):
    raw_scores = mix("sqkgd,stkd->skgqt", queries, key_rot) * HEAD_DIM ** (-0.5)
    causal = jnp.arange(SEQ_LEN)[:, None] >= jnp.arange(SEQ_LEN)[None, :]
    return jnp.where(causal, raw_scores, -jnp.inf)


def forward(stream, attn_weights, mlp_weights, gain_rows):
    w_query, w_key, w_value, w_out = attn_weights
    w_gate, w_up, w_down = mlp_weights
    row_count = stream.shape[0]
    seq_count = row_count // SEQ_LEN
    group_size = HEADS // KV_HEADS
    cosine, sine_tab = rope_tables()
    normed_one, inv_one, entry_one = norm_forward(stream, gain_rows[0])
    queries = matmul(entry_one, w_query).reshape(seq_count, SEQ_LEN, HEADS, HEAD_DIM)
    queries = (
        rotate(queries, cosine, sine_tab)
        .astype(jnp.bfloat16)
        .reshape(seq_count, SEQ_LEN, KV_HEADS, group_size, HEAD_DIM)
    )
    key_rot = rotate(
        matmul(entry_one, w_key).reshape(seq_count, SEQ_LEN, KV_HEADS, HEAD_DIM), cosine, sine_tab
    ).astype(jnp.bfloat16)
    values = (
        matmul(entry_one, w_value)
        .astype(jnp.bfloat16)
        .reshape(seq_count, SEQ_LEN, KV_HEADS, HEAD_DIM)
    )
    scores = scores_of(queries, key_rot)
    row_top = jnp.max(scores, axis=-1, keepdims=True)
    log_total = row_top + jnp.log(jnp.sum(jnp.exp(scores - row_top), axis=-1, keepdims=True))
    attn_probs = jnp.exp(scores - log_total).astype(jnp.bfloat16)
    context = (
        mix("skgqt,stkd->sqkgd", attn_probs, values).astype(jnp.bfloat16).reshape(row_count, D)
    )
    middle = stream + matmul(context, w_out)
    normed_two, inv_two, entry_two = norm_forward(middle, gain_rows[1])
    gate_pre = matmul(entry_two, w_gate)
    upward = matmul(entry_two, w_up)
    hidden = (jax.nn.silu(gate_pre) * upward).astype(jnp.bfloat16)
    output = middle + matmul(hidden, w_down)
    kept_state = (
        normed_one,
        inv_one,
        entry_one,
        queries,
        key_rot,
        values,
        log_total,
        context,
        normed_two,
        inv_two,
        entry_two,
        gate_pre,
        upward,
        hidden,
    )
    return (output, kept_state)


def mlp_backward(grad_out, kept_state, mlp_weights, gain_rows):
    normed_two, inv_two, entry_two, gate_pre, upward, hidden = kept_state[8:]
    w_gate, w_up, w_down = mlp_weights
    grad_bf = grad_out.astype(jnp.bfloat16)
    grad_down = inner(hidden, grad_bf)
    grad_hidden = outer_t(grad_bf, w_down)
    sigma = jax.nn.sigmoid(gate_pre)
    grad_gate = (grad_hidden * upward * sigma * (1.0 + gate_pre * (1.0 - sigma))).astype(
        jnp.bfloat16
    )
    grad_upward = (grad_hidden * gate_pre * sigma).astype(jnp.bfloat16)
    grad_gate_w = inner(entry_two, grad_gate)
    grad_up_w = inner(entry_two, grad_upward)
    grad_entry = outer_t(grad_gate, w_gate) + outer_t(grad_upward, w_up)
    grad_norm, gain_two = norm_backward(grad_entry, normed_two, inv_two, gain_rows[1])
    flat_grad = flatten([grad_gate_w, grad_up_w, grad_down])
    return (grad_out + grad_norm, flat_grad, gain_two)


def attn_backward(grad_middle, kept_state, attn_weights, gain_rows):
    normed_one, inv_one, entry_one, queries, key_rot, values, log_total, context = kept_state[:8]
    w_query, w_key, w_value, w_out = attn_weights
    row_count = grad_middle.shape[0]
    seq_count = row_count // SEQ_LEN
    group_size = HEADS // KV_HEADS
    kv_width = KV_HEADS * HEAD_DIM
    cosine, sine_tab = rope_tables()
    grad_bf = grad_middle.astype(jnp.bfloat16)
    grad_out_w = inner(context, grad_bf)
    grad_context = (
        outer_t(grad_bf, w_out)
        .astype(jnp.bfloat16)
        .reshape(seq_count, SEQ_LEN, KV_HEADS, group_size, HEAD_DIM)
    )
    soft_probs = jnp.exp(scores_of(queries, key_rot) - log_total)
    grad_soft = mix("sqkgd,stkd->skgqt", grad_context, values)
    row_dot = jnp.sum(soft_probs * grad_soft, axis=-1, keepdims=True)
    grad_scores = (soft_probs * (grad_soft - row_dot) * HEAD_DIM ** (-0.5)).astype(jnp.bfloat16)
    grad_query = mix("skgqt,stkd->sqkgd", grad_scores, key_rot).reshape(
        seq_count, SEQ_LEN, HEADS, HEAD_DIM
    )
    grad_query = rotate(grad_query, cosine, -sine_tab).astype(jnp.bfloat16).reshape(row_count, D)
    grad_key = (
        rotate(mix("skgqt,sqkgd->stkd", grad_scores, queries), cosine, -sine_tab)
        .astype(jnp.bfloat16)
        .reshape(row_count, kv_width)
    )
    grad_value = (
        mix("skgqt,sqkgd->stkd", soft_probs.astype(jnp.bfloat16), grad_context)
        .astype(jnp.bfloat16)
        .reshape(row_count, kv_width)
    )
    grad_entry = (
        outer_t(grad_query, w_query) + outer_t(grad_key, w_key) + outer_t(grad_value, w_value)
    )
    grad_norm, gain_one = norm_backward(grad_entry, normed_one, inv_one, gain_rows[0])
    flat_grad = flatten(
        [
            inner(entry_one, grad_query),
            inner(entry_one, grad_key),
            inner(entry_one, grad_value),
            grad_out_w,
        ]
    )
    return (grad_middle + grad_norm, flat_grad, gain_one)


def bit_count(devices):
    bits = devices.bit_length() - 1
    assert 1 << bits == devices
    return bits


def bit_orders(bits):
    plain = list(range(bits - 1, -1, -1))
    swapped = list(plain)
    if bits > 2:
        first, second = swapped.index(2), swapped.index(1)
        swapped[first], swapped[second] = swapped[second], swapped[first]
    return [plain if piece % 2 == 0 else swapped for piece in range(PIECES)]


def coordinates(bits):
    me = lax.axis_index("dp")
    digits = [lax.rem(me // (1 << bit), 2) for bit in range(bits)]
    partners = [me + (1 << bit) * (1 - 2 * digits[bit]) for bit in range(bits)]
    return digits, partners


def meet(partners):
    barrier = pltpu.get_barrier_semaphore()
    for partner in partners:
        pl.semaphore_signal(barrier, inc=1, device_id=(partner,), device_id_type=MESH)
    pl.semaphore_wait(barrier, len(partners))


def pick(bits, fixed):
    return tuple(fixed.get(bit, slice(None)) for bit in range(bits - 1, -1, -1))


def locate(piece):
    return (0, piece // 4) if piece % 4 == 0 else (1, piece - piece // 4 - 1)


def gather_kernel(bits, attn_ref, mlp_ref, attn_full, mlp_full, local_sem, send_sem, recv_sem):
    digits, partners = coordinates(bits)
    orders = bit_orders(bits)
    fulls = (attn_full, mlp_full)
    here = pick(bits, dict(enumerate(digits)))
    own = [
        pltpu.make_async_copy(shard, full.at[here], local_sem.at[number])
        for number, (shard, full) in enumerate(zip((attn_ref, mlp_ref), fulls))
    ]
    for copy in own:
        copy.start()
    meet(partners)
    for copy in own:
        copy.wait()
    flights = {}
    for stage in range(bits):
        for piece in range(PIECES):
            if stage > 0:
                flights[piece, stage - 1].wait_recv()
            order = orders[piece]
            fixed = {bit: digits[bit] for bit in order[stage:]}
            array, spot = locate(piece)
            block = fulls[array].at[pick(bits, fixed) + (spot,)]
            copy = pltpu.make_async_remote_copy(
                src_ref=block,
                dst_ref=block,
                send_sem=send_sem.at[piece, stage],
                recv_sem=recv_sem.at[piece, stage],
                device_id=(partners[order[stage]],),
                device_id_type=MESH,
            )
            copy.start()
            flights[piece, stage] = copy
    for piece in range(PIECES):
        flights[piece, bits - 1].wait_recv()
    for copy in flights.values():
        copy.wait_send()


def gather(attn_shard, mlp_shard):
    devices = lax.axis_size("dp")
    bits = bit_count(devices)
    attn = attn_shard.reshape(ATTN_PIECES, -1, LANES)
    mlp = mlp_shard.reshape(MLP_PIECES, -1, LANES)
    vmem = pl.BlockSpec(memory_space=pltpu.VMEM)
    attn_full, mlp_full = pl.pallas_call(
        lambda *refs: gather_kernel(bits, *refs),
        out_shape=tuple(
            jax.ShapeDtypeStruct((2,) * bits + part.shape, part.dtype) for part in (attn, mlp)
        ),
        in_specs=[vmem, vmem],
        out_specs=(vmem, vmem),
        scratch_shapes=[
            pltpu.SemaphoreType.DMA((2,)),
            pltpu.SemaphoreType.DMA((PIECES, bits)),
            pltpu.SemaphoreType.DMA((PIECES, bits)),
        ],
        compiler_params=pltpu.CompilerParams(
            collective_id=0, has_side_effects=True, vmem_limit_bytes=60 << 20
        ),
    )(attn, mlp)
    return attn_full.reshape(-1, LANES), mlp_full.reshape(-1, LANES)


def strided(start, size, stride):
    return pl.ds(start, size, stride=stride)


def low_half(shape):
    return lax.broadcasted_iota(jnp.int32, shape, 1) < LANES // 2


def swap_halves(block):
    return pltpu.roll(block, LANES // 2, axis=1)


def unflatten_one(flat_ref, first_row, wide, pair, out_ref):
    rows, columns = out_ref.shape
    blocks, rest = divmod(columns, LANES)

    @pl.loop(0, rows * columns // LANES // WIDEN)
    def _(step):
        start = pl.multiple_of(step * WIDEN, WIDEN)
        wide[pl.ds(start, WIDEN), :] = flat_ref[pl.ds(first_row + start, WIDEN), :].astype(
            jnp.float32
        )

    @pl.loop(0, rows // CHUNK)
    def _(step):
        base = step * (CHUNK * columns // LANES)
        target = pl.ds(pl.multiple_of(step * CHUNK, CHUNK), CHUNK)
        if rest == 0:
            for block in range(blocks):
                out_ref[target, block * LANES : (block + 1) * LANES] = wide[
                    strided(base + block, CHUNK, blocks), :
                ].astype(jnp.bfloat16)
        else:
            period, half = 2 * blocks + 1, CHUNK // 2
            lines = [wide[strided(base + line, half, period), :] for line in range(period)]
            turned = [swap_halves(line) for line in lines[blocks:]]
            low = low_half((half, LANES))
            for block in range(blocks + 1):
                odd = turned[block]
                if block < blocks:
                    odd = jnp.where(low, odd, turned[block + 1])
                pair[block, strided(0, half, 2), :] = lines[block]
                pair[block, strided(1, half, 2), :] = odd
            for block in range(blocks):
                out_ref[target, block * LANES : (block + 1) * LANES] = pair[block].astype(
                    jnp.bfloat16
                )
            out_ref[target, blocks * LANES :] = pair[blocks][:, :rest].astype(jnp.bfloat16)


def flatten_one(grad_ref, first_row, wide, pair, flat_ref):
    rows, columns = grad_ref.shape
    blocks, rest = divmod(columns, LANES)

    @pl.loop(0, rows // CHUNK)
    def _(step):
        base = step * (CHUNK * columns // LANES)
        origin = pl.ds(pl.multiple_of(step * CHUNK, CHUNK), CHUNK)
        if rest == 0:
            for block in range(blocks):
                wide[strided(base + block, CHUNK, blocks), :] = grad_ref[
                    origin, block * LANES : (block + 1) * LANES
                ].astype(jnp.float32)
        else:
            period, half = 2 * blocks + 1, CHUNK // 2
            for block in range(blocks):
                pair[block] = grad_ref[origin, block * LANES : (block + 1) * LANES].astype(
                    jnp.float32
                )
            tail = grad_ref[origin, blocks * LANES :].astype(jnp.float32)
            pair[blocks] = jnp.concatenate([tail, tail], axis=1)
            even = [pair[block, strided(0, half, 2), :] for block in range(blocks + 1)]
            turned = [
                swap_halves(pair[block, strided(1, half, 2), :]) for block in range(blocks + 1)
            ]
            low = low_half((half, LANES))
            lines = even[:blocks] + [jnp.where(low, even[blocks], turned[0])]
            lines += [
                jnp.where(low, turned[block], turned[block + 1]) for block in range(blocks)
            ]
            for line in range(period):
                wide[strided(base + line, half, period), :] = lines[line]

    @pl.loop(0, rows * columns // LANES // WIDEN)
    def _(step):
        start = pl.multiple_of(step * WIDEN, WIDEN)
        flat_ref[pl.ds(first_row + start, WIDEN), :] = wide[pl.ds(start, WIDEN), :].astype(
            jnp.bfloat16
        )


KV_WIDTH = KV_HEADS * HEAD_DIM
ATTN_SHAPES = ((D, D), (D, KV_WIDTH), (D, KV_WIDTH), (D, D))
MLP_SHAPES = ((D, FF), (D, FF), (FF, D))


def relayout_scratch():
    longest = max(rows * columns for rows, columns in ATTN_SHAPES + MLP_SHAPES) // LANES
    widest = max(columns for _, columns in ATTN_SHAPES + MLP_SHAPES) // LANES + 1
    return [
        pltpu.VMEM((longest, LANES), jnp.float32),
        pltpu.VMEM((widest, CHUNK, LANES), jnp.float32),
    ]


def relayout(one, shapes, to_flat):
    def kernel(*refs):
        wide, pair = refs[-2:]
        flat_ref = refs[-3] if to_flat else refs[0]
        matrices = refs[:-3] if to_flat else refs[1:-2]
        first_row = 0
        for matrix in matrices:
            one(*((matrix, first_row, wide, pair, flat_ref) if to_flat else
                  (flat_ref, first_row, wide, pair, matrix)))
            first_row += matrix.shape[0] * matrix.shape[1] // LANES

    vmem = pl.BlockSpec(memory_space=pltpu.VMEM)
    total = sum(rows * columns for rows, columns in shapes) // LANES
    flat = jax.ShapeDtypeStruct((total, LANES), jnp.bfloat16)
    many = tuple(jax.ShapeDtypeStruct(shape, jnp.bfloat16) for shape in shapes)
    return pl.pallas_call(
        kernel,
        out_shape=flat if to_flat else many,
        in_specs=[vmem] * (len(shapes) if to_flat else 1),
        out_specs=vmem if to_flat else (vmem,) * len(shapes),
        scratch_shapes=relayout_scratch(),
        compiler_params=pltpu.CompilerParams(vmem_limit_bytes=40 << 20),
    )


def unflatten(flat, shapes):
    return relayout(unflatten_one, shapes, False)(flat)


def flatten(grads):
    shapes = tuple(grad.shape for grad in grads)
    return relayout(flatten_one, shapes, True)(*[grad.astype(jnp.bfloat16) for grad in grads])


def scatter_kernel(bits, attn_ref, mlp_ref, gain_ref, attn_out, mlp_out, gain_out, *scratch):
    totals = (attn_ref, mlp_ref)
    outs = (attn_out, mlp_out)
    landing = scratch[:bits]
    held = scratch[bits : 2 * bits - 1]
    gain_sent, gain_landing = scratch[2 * bits - 1 : 2 * bits + 1]
    send_sem, recv_sem, gain_send, gain_recv = scratch[2 * bits + 1 :]
    digits, partners = coordinates(bits)
    orders = [order[::-1] for order in bit_orders(bits)]
    meet(partners)
    flights = {}
    gain_flights = {}

    def block_index(order, stage, digit):
        if stage == 0:
            return pick(bits, {order[0]: digit})
        left = [bit for bit in range(bits - 1, -1, -1) if bit not in order[:stage]]
        return tuple(digit if bit == order[stage] else slice(None) for bit in left)

    def launch(piece, stage):
        order = orders[piece]
        bit = order[stage]
        lead = block_index(order, stage, 1 - digits[bit])
        if stage == 0:
            array, place = locate(piece)
            src = totals[array].at[lead + (place,)]
        else:
            src = held[stage - 1].at[(piece,) + lead]
        copy = pltpu.make_async_remote_copy(
            src_ref=src,
            dst_ref=landing[stage].at[piece],
            send_sem=send_sem.at[piece, stage],
            recv_sem=recv_sem.at[piece, stage],
            device_id=(partners[bit],),
            device_id_type=MESH,
        )
        copy.start()
        flights[piece, stage] = copy

    def absorb(piece, stage):
        flights[piece, stage].wait_recv()
        order = orders[piece]
        bit = order[stage]
        lead = block_index(order, stage, digits[bit])
        free = len(lead) - 1
        array, slot = locate(piece)
        for number in range(1 << free):
            picks = [(number >> place) & 1 for place in range(free - 1, -1, -1)]
            spot = iter(picks)
            where = tuple(next(spot) if isinstance(item, slice) else item for item in lead)
            if stage == 0:
                mine = totals[array][where + (slot,)]
            else:
                mine = held[stage - 1][(piece,) + where]
            other = landing[stage][(piece,) + tuple(picks)]
            value = mine.astype(jnp.float32) + other.astype(jnp.float32)
            if stage == bits - 1:
                outs[array][slot] = value
            else:
                held[stage][(piece,) + tuple(picks)] = value.astype(jnp.bfloat16)

    def launch_gain(stage):
        copy = pltpu.make_async_remote_copy(
            src_ref=gain_ref if stage == 0 else gain_sent.at[stage],
            dst_ref=gain_landing.at[stage],
            send_sem=gain_send.at[stage],
            recv_sem=gain_recv.at[stage],
            device_id=(partners[stage],),
            device_id_type=MESH,
        )
        copy.start()
        gain_flights[stage] = copy

    def absorb_gain(stage):
        gain_flights[stage].wait_recv()
        mine = gain_ref[...] if stage == 0 else gain_sent[stage]
        value = mine + gain_landing[stage]
        if stage == bits - 1:
            gain_out[...] = value
        else:
            gain_sent[stage + 1] = value

    for stage in range(bits):
        if stage > 0:
            absorb_gain(stage - 1)
        launch_gain(stage)
        for piece in range(PIECES):
            if stage > 0:
                absorb(piece, stage - 1)
            launch(piece, stage)
    absorb_gain(bits - 1)
    for piece in range(PIECES):
        absorb(piece, bits - 1)
    for copy in list(flights.values()) + list(gain_flights.values()):
        copy.wait_send()


def scatter(attn_flat, mlp_flat, gains):
    devices = lax.axis_size("dp")
    bits = bit_count(devices)
    attn = attn_flat.reshape((2,) * bits + (ATTN_PIECES, -1, LANES))
    mlp = mlp_flat.reshape((2,) * bits + (MLP_PIECES, -1, LANES))
    rows = mlp.shape[-2]
    slots = [(PIECES,) + (2,) * (bits - 1 - stage) + (rows, LANES) for stage in range(bits)]
    vmem = pl.BlockSpec(memory_space=pltpu.VMEM)
    attn_sum, mlp_sum, gain_sum = pl.pallas_call(
        lambda *refs: scatter_kernel(bits, *refs),
        out_shape=(
            jax.ShapeDtypeStruct((ATTN_PIECES, rows, LANES), jnp.float32),
            jax.ShapeDtypeStruct((MLP_PIECES, rows, LANES), jnp.float32),
            jax.ShapeDtypeStruct(gains.shape, jnp.float32),
        ),
        in_specs=[vmem] * 3,
        out_specs=(vmem,) * 3,
        scratch_shapes=[pltpu.VMEM(slot, jnp.bfloat16) for slot in slots]
        + [pltpu.VMEM(slot, jnp.bfloat16) for slot in slots[:-1]]
        + [
            pltpu.VMEM((bits,) + gains.shape, jnp.float32),
            pltpu.VMEM((bits,) + gains.shape, jnp.float32),
            pltpu.SemaphoreType.DMA((PIECES, bits)),
            pltpu.SemaphoreType.DMA((PIECES, bits)),
            pltpu.SemaphoreType.DMA((bits,)),
            pltpu.SemaphoreType.DMA((bits,)),
        ],
        compiler_params=pltpu.CompilerParams(
            collective_id=1, has_side_effects=True, vmem_limit_bytes=60 << 20
        ),
    )(attn, mlp, gains)
    return attn_sum.reshape(-1), mlp_sum.reshape(-1), gain_sum


def body(inputs, cotangent, attn_shard, mlp_shard, gain_rows):
    attn_full, mlp_full = gather(attn_shard, mlp_shard)
    attn_weights = unflatten(attn_full, ATTN_SHAPES)
    mlp_weights = unflatten(mlp_full, MLP_SHAPES)
    outputs, kept_state = forward(inputs, attn_weights, mlp_weights, gain_rows)
    grad_middle, mlp_flat, gain_two = mlp_backward(cotangent, kept_state, mlp_weights, gain_rows)
    grad_input, attn_flat, gain_one = attn_backward(
        grad_middle, kept_state, attn_weights, gain_rows
    )
    gains = jnp.stack([gain_one, gain_two])
    attn_grad, mlp_grad, gain_grad = scatter(attn_flat, mlp_flat, gains)
    return (outputs, grad_input, attn_grad, mlp_grad, gain_grad)


def solution(mesh):
    placed = (P("dp", None), P("dp", None), P("dp"), P("dp"), P())
    return jax.shard_map(
        body,
        mesh=mesh,
        in_specs=placed,
        out_specs=(P("dp", None), P("dp", None), P("dp"), P("dp"), P()),
        check_vma=False,
    )
```

```python
import jax
import jax.numpy as jnp
from jax import lax
from jax.experimental import pallas as pl
from jax.experimental.pallas import tpu as pltpu
from jax.sharding import PartitionSpec as P

LANES = 128
ATTN_PIECES = 3
MLP_PIECES = 9
PIECES = ATTN_PIECES + MLP_PIECES
CHUNK = 96
WIDEN = 288
MESH = pl.DeviceIdType.MESH

D = 576
HEADS = 9
KV_HEADS = 3
HEAD_DIM = 64
FF = 1536
SEQ_LEN = 192


EPS = 1e-05
THETA = 100000.0


def mix(form, left, right):
    return jnp.einsum(form, left, right, preferred_element_type=jnp.float32)


def matmul(left, right):
    return jnp.dot(left, right, preferred_element_type=jnp.float32)


def inner(left, right):
    return lax.dot_general(
        left, right, (((0,), (0,)), ((), ())), preferred_element_type=jnp.float32
    )


def outer_t(left, right):
    return lax.dot_general(
        left, right, (((1,), (1,)), ((), ())), preferred_element_type=jnp.float32
    )


def split_attention(flat):
    kv_width = KV_HEADS * HEAD_DIM
    edge_one = D * D
    edge_two = edge_one + D * kv_width
    edge_three = edge_two + D * kv_width
    return (
        flat[:edge_one].reshape(D, D),
        flat[edge_one:edge_two].reshape(D, kv_width),
        flat[edge_two:edge_three].reshape(D, kv_width),
        flat[edge_three:].reshape(D, D),
    )


def split_mlp(flat):
    edge_one = D * FF
    return (
        flat[:edge_one].reshape(D, FF),
        flat[edge_one : 2 * edge_one].reshape(D, FF),
        flat[2 * edge_one :].reshape(FF, D),
    )


def rope_tables():
    position = jnp.arange(SEQ_LEN).astype(jnp.float32)
    frequency = THETA ** (-(jnp.arange(HEAD_DIM // 2).astype(jnp.float32) * 2.0 / HEAD_DIM))
    angles = position[:, None] * frequency[None, :]
    return (jnp.cos(angles), jnp.sin(angles))


def rotate(tensor, cosine, sine_tab):
    half_dim = tensor.shape[-1] // 2
    lower_half = tensor[..., :half_dim]
    upper_half = tensor[..., half_dim:]
    cos_wide = cosine[None, :, None, :]
    sin_wide = sine_tab[None, :, None, :]
    return jnp.concatenate(
        [
            lower_half * cos_wide - upper_half * sin_wide,
            upper_half * cos_wide + lower_half * sin_wide,
        ],
        axis=-1,
    )


def norm_forward(stream, gain_row):
    inv_rms = lax.rsqrt(jnp.mean(stream * stream, axis=-1, keepdims=True) + EPS)
    normed = stream * inv_rms
    return (normed, inv_rms, (normed * gain_row).astype(jnp.bfloat16))


def norm_backward(grad_in, normed, inv_rms, gain_row):
    scaled = grad_in * gain_row
    grad_stream = inv_rms * (scaled - normed * jnp.mean(scaled * normed, axis=-1, keepdims=True))
    return (grad_stream, jnp.sum(grad_in * normed, axis=0))


def scores_of(queries, key_rot):
    raw_scores = mix("sqkgd,stkd->skgqt", queries, key_rot) * HEAD_DIM ** (-0.5)
    causal = jnp.arange(SEQ_LEN)[:, None] >= jnp.arange(SEQ_LEN)[None, :]
    return jnp.where(causal, raw_scores, -jnp.inf)


def forward(stream, attn_weights, mlp_weights, gain_rows):
    w_query, w_key, w_value, w_out = attn_weights
    w_gate, w_up, w_down = mlp_weights
    row_count = stream.shape[0]
    seq_count = row_count // SEQ_LEN
    group_size = HEADS // KV_HEADS
    cosine, sine_tab = rope_tables()
    normed_one, inv_one, entry_one = norm_forward(stream, gain_rows[0])
    queries = matmul(entry_one, w_query).reshape(seq_count, SEQ_LEN, HEADS, HEAD_DIM)
    queries = (
        rotate(queries, cosine, sine_tab)
        .astype(jnp.bfloat16)
        .reshape(seq_count, SEQ_LEN, KV_HEADS, group_size, HEAD_DIM)
    )
    key_rot = rotate(
        matmul(entry_one, w_key).reshape(seq_count, SEQ_LEN, KV_HEADS, HEAD_DIM), cosine, sine_tab
    ).astype(jnp.bfloat16)
    values = (
        matmul(entry_one, w_value)
        .astype(jnp.bfloat16)
        .reshape(seq_count, SEQ_LEN, KV_HEADS, HEAD_DIM)
    )
    scores = scores_of(queries, key_rot)
    row_top = jnp.max(scores, axis=-1, keepdims=True)
    log_total = row_top + jnp.log(jnp.sum(jnp.exp(scores - row_top), axis=-1, keepdims=True))
    attn_probs = jnp.exp(scores - log_total).astype(jnp.bfloat16)
    context = (
        mix("skgqt,stkd->sqkgd", attn_probs, values).astype(jnp.bfloat16).reshape(row_count, D)
    )
    middle = stream + matmul(context, w_out)
    normed_two, inv_two, entry_two = norm_forward(middle, gain_rows[1])
    gate_pre = matmul(entry_two, w_gate)
    upward = matmul(entry_two, w_up)
    hidden = (jax.nn.silu(gate_pre) * upward).astype(jnp.bfloat16)
    output = middle + matmul(hidden, w_down)
    kept_state = (
        normed_one,
        inv_one,
        entry_one,
        queries,
        key_rot,
        values,
        log_total,
        context,
        normed_two,
        inv_two,
        entry_two,
        gate_pre,
        upward,
        hidden,
    )
    return (output, kept_state)


def mlp_backward(grad_out, kept_state, mlp_weights, gain_rows):
    normed_two, inv_two, entry_two, gate_pre, upward, hidden = kept_state[8:]
    w_gate, w_up, w_down = mlp_weights
    grad_bf = grad_out.astype(jnp.bfloat16)
    grad_down = inner(hidden, grad_bf)
    grad_hidden = outer_t(grad_bf, w_down)
    sigma = jax.nn.sigmoid(gate_pre)
    grad_gate = (grad_hidden * upward * sigma * (1.0 + gate_pre * (1.0 - sigma))).astype(
        jnp.bfloat16
    )
    grad_upward = (grad_hidden * gate_pre * sigma).astype(jnp.bfloat16)
    grad_gate_w = inner(entry_two, grad_gate)
    grad_up_w = inner(entry_two, grad_upward)
    grad_entry = outer_t(grad_gate, w_gate) + outer_t(grad_upward, w_up)
    grad_norm, gain_two = norm_backward(grad_entry, normed_two, inv_two, gain_rows[1])
    flat_grad = flatten([grad_gate_w, grad_up_w, grad_down])
    return (grad_out + grad_norm, flat_grad, gain_two)


def attn_backward(grad_middle, kept_state, attn_weights, gain_rows):
    normed_one, inv_one, entry_one, queries, key_rot, values, log_total, context = kept_state[:8]
    w_query, w_key, w_value, w_out = attn_weights
    row_count = grad_middle.shape[0]
    seq_count = row_count // SEQ_LEN
    group_size = HEADS // KV_HEADS
    kv_width = KV_HEADS * HEAD_DIM
    cosine, sine_tab = rope_tables()
    grad_bf = grad_middle.astype(jnp.bfloat16)
    grad_out_w = inner(context, grad_bf)
    grad_context = (
        outer_t(grad_bf, w_out)
        .astype(jnp.bfloat16)
        .reshape(seq_count, SEQ_LEN, KV_HEADS, group_size, HEAD_DIM)
    )
    soft_probs = jnp.exp(scores_of(queries, key_rot) - log_total)
    grad_soft = mix("sqkgd,stkd->skgqt", grad_context, values)
    row_dot = jnp.sum(soft_probs * grad_soft, axis=-1, keepdims=True)
    grad_scores = (soft_probs * (grad_soft - row_dot) * HEAD_DIM ** (-0.5)).astype(jnp.bfloat16)
    grad_query = mix("skgqt,stkd->sqkgd", grad_scores, key_rot).reshape(
        seq_count, SEQ_LEN, HEADS, HEAD_DIM
    )
    grad_query = rotate(grad_query, cosine, -sine_tab).astype(jnp.bfloat16).reshape(row_count, D)
    grad_key = (
        rotate(mix("skgqt,sqkgd->stkd", grad_scores, queries), cosine, -sine_tab)
        .astype(jnp.bfloat16)
        .reshape(row_count, kv_width)
    )
    grad_value = (
        mix("skgqt,sqkgd->stkd", soft_probs.astype(jnp.bfloat16), grad_context)
        .astype(jnp.bfloat16)
        .reshape(row_count, kv_width)
    )
    grad_entry = (
        outer_t(grad_query, w_query) + outer_t(grad_key, w_key) + outer_t(grad_value, w_value)
    )
    grad_norm, gain_one = norm_backward(grad_entry, normed_one, inv_one, gain_rows[0])
    flat_grad = flatten(
        [
            inner(entry_one, grad_query),
            inner(entry_one, grad_key),
            inner(entry_one, grad_value),
            grad_out_w,
        ]
    )
    return (grad_middle + grad_norm, flat_grad, gain_one)


def bit_count(devices):
    bits = devices.bit_length() - 1
    assert 1 << bits == devices
    return bits


def bit_orders(bits):
    upper = list(range(bits - 1, 2, -1))
    if bits < 3:
        return [list(range(bits - 1, -1, -1))] * PIECES
    late, early = upper + [2, 1, 0], upper + [1, 2, 0]
    one, two = [1] + upper + [2, 0], [2] + upper + [1, 0]
    cycle = (late, one, two, early, one, two)
    return [cycle[piece % len(cycle)] for piece in range(PIECES)]


def coordinates(bits):
    me = lax.axis_index("dp")
    digits = [lax.rem(me // (1 << bit), 2) for bit in range(bits)]
    partners = [me + (1 << bit) * (1 - 2 * digits[bit]) for bit in range(bits)]
    return digits, partners


def meet(partners):
    barrier = pltpu.get_barrier_semaphore()
    for partner in partners:
        pl.semaphore_signal(barrier, inc=1, device_id=(partner,), device_id_type=MESH)
    pl.semaphore_wait(barrier, len(partners))


def pick(bits, fixed):
    return tuple(fixed.get(bit, slice(None)) for bit in range(bits - 1, -1, -1))


def locate(piece):
    return (0, piece // 4) if piece % 4 == 0 else (1, piece - piece // 4 - 1)


def gather_kernel(bits, attn_ref, mlp_ref, attn_full, mlp_full, local_sem, send_sem, recv_sem):
    digits, partners = coordinates(bits)
    orders = bit_orders(bits)
    fulls = (attn_full, mlp_full)
    here = pick(bits, dict(enumerate(digits)))
    own = [
        pltpu.make_async_copy(shard, full.at[here], local_sem.at[number])
        for number, (shard, full) in enumerate(zip((attn_ref, mlp_ref), fulls))
    ]
    for copy in own:
        copy.start()
    meet(partners)
    for copy in own:
        copy.wait()
    flights = {}
    for stage in range(bits):
        for piece in range(PIECES):
            if stage > 0:
                flights[piece, stage - 1].wait_recv()
            order = orders[piece]
            fixed = {bit: digits[bit] for bit in order[stage:]}
            array, spot = locate(piece)
            block = fulls[array].at[pick(bits, fixed) + (spot,)]
            copy = pltpu.make_async_remote_copy(
                src_ref=block,
                dst_ref=block,
                send_sem=send_sem.at[piece, stage],
                recv_sem=recv_sem.at[piece, stage],
                device_id=(partners[order[stage]],),
                device_id_type=MESH,
            )
            copy.start()
            flights[piece, stage] = copy
    for piece in range(PIECES):
        flights[piece, bits - 1].wait_recv()
    for copy in flights.values():
        copy.wait_send()


def gather(attn_shard, mlp_shard):
    devices = lax.axis_size("dp")
    bits = bit_count(devices)
    attn = attn_shard.reshape(ATTN_PIECES, -1, LANES)
    mlp = mlp_shard.reshape(MLP_PIECES, -1, LANES)
    vmem = pl.BlockSpec(memory_space=pltpu.VMEM)
    attn_full, mlp_full = pl.pallas_call(
        lambda *refs: gather_kernel(bits, *refs),
        out_shape=tuple(
            jax.ShapeDtypeStruct((2,) * bits + part.shape, part.dtype) for part in (attn, mlp)
        ),
        in_specs=[vmem, vmem],
        out_specs=(vmem, vmem),
        scratch_shapes=[
            pltpu.SemaphoreType.DMA((2,)),
            pltpu.SemaphoreType.DMA((PIECES, bits)),
            pltpu.SemaphoreType.DMA((PIECES, bits)),
        ],
        compiler_params=pltpu.CompilerParams(
            collective_id=0, has_side_effects=True, vmem_limit_bytes=16 << 20
        ),
    )(attn, mlp)
    return attn_full.reshape(-1, LANES), mlp_full.reshape(-1, LANES)


def strided(start, size, stride):
    return pl.ds(start, size, stride=stride)


def low_half(shape):
    return lax.broadcasted_iota(jnp.int32, shape, 1) < LANES // 2


def swap_halves(block):
    return pltpu.roll(block, LANES // 2, axis=1)


def unflatten_one(flat_ref, first_row, wide, pair, out_ref):
    rows, columns = out_ref.shape
    blocks, rest = divmod(columns, LANES)

    @pl.loop(0, rows * columns // LANES // WIDEN)
    def _(step):
        start = pl.multiple_of(step * WIDEN, WIDEN)
        wide[pl.ds(start, WIDEN), :] = flat_ref[pl.ds(first_row + start, WIDEN), :].astype(
            jnp.float32
        )

    @pl.loop(0, rows // CHUNK)
    def _(step):
        base = step * (CHUNK * columns // LANES)
        target = pl.ds(pl.multiple_of(step * CHUNK, CHUNK), CHUNK)
        if rest == 0:
            for block in range(blocks):
                out_ref[target, block * LANES : (block + 1) * LANES] = wide[
                    strided(base + block, CHUNK, blocks), :
                ].astype(jnp.bfloat16)
        else:
            period, half = 2 * blocks + 1, CHUNK // 2
            lines = [wide[strided(base + line, half, period), :] for line in range(period)]
            turned = [swap_halves(line) for line in lines[blocks:]]
            low = low_half((half, LANES))
            for block in range(blocks + 1):
                odd = turned[block]
                if block < blocks:
                    odd = jnp.where(low, odd, turned[block + 1])
                pair[block, strided(0, half, 2), :] = lines[block]
                pair[block, strided(1, half, 2), :] = odd
            for block in range(blocks):
                out_ref[target, block * LANES : (block + 1) * LANES] = pair[block].astype(
                    jnp.bfloat16
                )
            out_ref[target, blocks * LANES :] = pair[blocks][:, :rest].astype(jnp.bfloat16)


def flatten_one(grad_ref, first_row, wide, pair, flat_ref):
    rows, columns = grad_ref.shape
    blocks, rest = divmod(columns, LANES)

    @pl.loop(0, rows // CHUNK)
    def _(step):
        base = step * (CHUNK * columns // LANES)
        origin = pl.ds(pl.multiple_of(step * CHUNK, CHUNK), CHUNK)
        if rest == 0:
            for block in range(blocks):
                wide[strided(base + block, CHUNK, blocks), :] = grad_ref[
                    origin, block * LANES : (block + 1) * LANES
                ].astype(jnp.float32)
        else:
            period, half = 2 * blocks + 1, CHUNK // 2
            for block in range(blocks):
                pair[block] = grad_ref[origin, block * LANES : (block + 1) * LANES].astype(
                    jnp.float32
                )
            tail = grad_ref[origin, blocks * LANES :].astype(jnp.float32)
            pair[blocks] = jnp.concatenate([tail, tail], axis=1)
            even = [pair[block, strided(0, half, 2), :] for block in range(blocks + 1)]
            turned = [
                swap_halves(pair[block, strided(1, half, 2), :]) for block in range(blocks + 1)
            ]
            low = low_half((half, LANES))
            lines = even[:blocks] + [jnp.where(low, even[blocks], turned[0])]
            lines += [
                jnp.where(low, turned[block], turned[block + 1]) for block in range(blocks)
            ]
            for line in range(period):
                wide[strided(base + line, half, period), :] = lines[line]

    @pl.loop(0, rows * columns // LANES // WIDEN)
    def _(step):
        start = pl.multiple_of(step * WIDEN, WIDEN)
        flat_ref[pl.ds(first_row + start, WIDEN), :] = wide[pl.ds(start, WIDEN), :].astype(
            jnp.bfloat16
        )


KV_WIDTH = KV_HEADS * HEAD_DIM
ATTN_SHAPES = ((D, D), (D, KV_WIDTH), (D, KV_WIDTH), (D, D))
MLP_SHAPES = ((D, FF), (D, FF), (FF, D))


def relayout_scratch():
    longest = max(rows * columns for rows, columns in ATTN_SHAPES + MLP_SHAPES) // LANES
    widest = max(columns for _, columns in ATTN_SHAPES + MLP_SHAPES) // LANES + 1
    return [
        pltpu.VMEM((longest, LANES), jnp.float32),
        pltpu.VMEM((widest, CHUNK, LANES), jnp.float32),
    ]


def relayout(one, shapes, to_flat):
    def kernel(*refs):
        wide, pair = refs[-2:]
        flat_ref = refs[-3] if to_flat else refs[0]
        matrices = refs[:-3] if to_flat else refs[1:-2]
        first_row = 0
        for matrix in matrices:
            one(*((matrix, first_row, wide, pair, flat_ref) if to_flat else
                  (flat_ref, first_row, wide, pair, matrix)))
            first_row += matrix.shape[0] * matrix.shape[1] // LANES

    vmem = pl.BlockSpec(memory_space=pltpu.VMEM)
    total = sum(rows * columns for rows, columns in shapes) // LANES
    flat = jax.ShapeDtypeStruct((total, LANES), jnp.bfloat16)
    many = tuple(jax.ShapeDtypeStruct(shape, jnp.bfloat16) for shape in shapes)
    return pl.pallas_call(
        kernel,
        out_shape=flat if to_flat else many,
        in_specs=[vmem] * (len(shapes) if to_flat else 1),
        out_specs=vmem if to_flat else (vmem,) * len(shapes),
        scratch_shapes=relayout_scratch(),
        compiler_params=pltpu.CompilerParams(vmem_limit_bytes=20 << 20),
    )


def unflatten(flat, shapes):
    return relayout(unflatten_one, shapes, False)(flat)


def flatten(grads):
    shapes = tuple(grad.shape for grad in grads)
    return relayout(flatten_one, shapes, True)(*[grad.astype(jnp.bfloat16) for grad in grads])


def scatter_kernel(bits, attn_ref, mlp_ref, gain_ref, attn_out, mlp_out, gain_out, *scratch):
    totals = (attn_ref, mlp_ref)
    outs = (attn_out, mlp_out)
    landing = scratch[:bits]
    held = scratch[bits : 2 * bits - 1]
    gain_sent, gain_landing = scratch[2 * bits - 1 : 2 * bits + 1]
    send_sem, recv_sem, gain_send, gain_recv = scratch[2 * bits + 1 :]
    digits, partners = coordinates(bits)
    orders = [order[::-1] for order in bit_orders(bits)]
    meet(partners)
    flights = {}
    gain_flights = {}

    def block_index(order, stage, digit):
        if stage == 0:
            return pick(bits, {order[0]: digit})
        left = [bit for bit in range(bits - 1, -1, -1) if bit not in order[:stage]]
        return tuple(digit if bit == order[stage] else slice(None) for bit in left)

    def launch(piece, stage):
        order = orders[piece]
        bit = order[stage]
        lead = block_index(order, stage, 1 - digits[bit])
        if stage == 0:
            array, place = locate(piece)
            src = totals[array].at[lead + (place,)]
        else:
            src = held[stage - 1].at[(piece,) + lead]
        copy = pltpu.make_async_remote_copy(
            src_ref=src,
            dst_ref=landing[stage].at[piece],
            send_sem=send_sem.at[piece, stage],
            recv_sem=recv_sem.at[piece, stage],
            device_id=(partners[bit],),
            device_id_type=MESH,
        )
        copy.start()
        flights[piece, stage] = copy

    def absorb(piece, stage):
        flights[piece, stage].wait_recv()
        order = orders[piece]
        bit = order[stage]
        lead = block_index(order, stage, digits[bit])
        free = len(lead) - 1
        array, slot = locate(piece)
        for number in range(1 << free):
            picks = [(number >> place) & 1 for place in range(free - 1, -1, -1)]
            spot = iter(picks)
            where = tuple(next(spot) if isinstance(item, slice) else item for item in lead)
            if stage == 0:
                mine = totals[array][where + (slot,)]
            else:
                mine = held[stage - 1][(piece,) + where]
            other = landing[stage][(piece,) + tuple(picks)]
            value = mine.astype(jnp.float32) + other.astype(jnp.float32)
            if stage == bits - 1:
                outs[array][slot] = value
            else:
                held[stage][(piece,) + tuple(picks)] = value.astype(jnp.bfloat16)

    def launch_gain(stage):
        copy = pltpu.make_async_remote_copy(
            src_ref=gain_ref if stage == 0 else gain_sent.at[stage],
            dst_ref=gain_landing.at[stage],
            send_sem=gain_send.at[stage],
            recv_sem=gain_recv.at[stage],
            device_id=(partners[stage],),
            device_id_type=MESH,
        )
        copy.start()
        gain_flights[stage] = copy

    def absorb_gain(stage):
        gain_flights[stage].wait_recv()
        mine = gain_ref[...] if stage == 0 else gain_sent[stage]
        value = mine + gain_landing[stage]
        if stage == bits - 1:
            gain_out[...] = value
        else:
            gain_sent[stage + 1] = value

    for stage in range(bits):
        if stage > 0:
            absorb_gain(stage - 1)
        launch_gain(stage)
        for piece in range(PIECES):
            if stage > 0:
                absorb(piece, stage - 1)
            launch(piece, stage)
    absorb_gain(bits - 1)
    for piece in range(PIECES):
        absorb(piece, bits - 1)
    for copy in list(flights.values()) + list(gain_flights.values()):
        copy.wait_send()


def scatter(attn_flat, mlp_flat, gains):
    devices = lax.axis_size("dp")
    bits = bit_count(devices)
    attn = attn_flat.reshape((2,) * bits + (ATTN_PIECES, -1, LANES))
    mlp = mlp_flat.reshape((2,) * bits + (MLP_PIECES, -1, LANES))
    rows = mlp.shape[-2]
    slots = [(PIECES,) + (2,) * (bits - 1 - stage) + (rows, LANES) for stage in range(bits)]
    vmem = pl.BlockSpec(memory_space=pltpu.VMEM)
    attn_sum, mlp_sum, gain_sum = pl.pallas_call(
        lambda *refs: scatter_kernel(bits, *refs),
        out_shape=(
            jax.ShapeDtypeStruct((ATTN_PIECES, rows, LANES), jnp.float32),
            jax.ShapeDtypeStruct((MLP_PIECES, rows, LANES), jnp.float32),
            jax.ShapeDtypeStruct(gains.shape, jnp.float32),
        ),
        in_specs=[vmem] * 3,
        out_specs=(vmem,) * 3,
        scratch_shapes=[pltpu.VMEM(slot, jnp.bfloat16) for slot in slots]
        + [pltpu.VMEM(slot, jnp.bfloat16) for slot in slots[:-1]]
        + [
            pltpu.VMEM((bits,) + gains.shape, jnp.float32),
            pltpu.VMEM((bits,) + gains.shape, jnp.float32),
            pltpu.SemaphoreType.DMA((PIECES, bits)),
            pltpu.SemaphoreType.DMA((PIECES, bits)),
            pltpu.SemaphoreType.DMA((bits,)),
            pltpu.SemaphoreType.DMA((bits,)),
        ],
        compiler_params=pltpu.CompilerParams(
            collective_id=1, has_side_effects=True, vmem_limit_bytes=32 << 20
        ),
    )(attn, mlp, gains)
    return attn_sum.reshape(-1), mlp_sum.reshape(-1), gain_sum


def body(inputs, cotangent, attn_shard, mlp_shard, gain_rows):
    attn_full, mlp_full = gather(attn_shard, mlp_shard)
    attn_weights = unflatten(attn_full, ATTN_SHAPES)
    mlp_weights = unflatten(mlp_full, MLP_SHAPES)
    outputs, kept_state = forward(inputs, attn_weights, mlp_weights, gain_rows)
    grad_middle, mlp_flat, gain_two = mlp_backward(cotangent, kept_state, mlp_weights, gain_rows)
    grad_input, attn_flat, gain_one = attn_backward(
        grad_middle, kept_state, attn_weights, gain_rows
    )
    gains = jnp.stack([gain_one, gain_two])
    attn_grad, mlp_grad, gain_grad = scatter(attn_flat, mlp_flat, gains)
    return (outputs, grad_input, attn_grad, mlp_grad, gain_grad)


def solution(mesh):
    placed = (P("dp", None), P("dp", None), P("dp"), P("dp"), P())
    return jax.shard_map(
        body,
        mesh=mesh,
        in_specs=placed,
        out_specs=(P("dp", None), P("dp", None), P("dp"), P("dp"), P()),
        check_vma=False,
    )
```

```python
import jax
import jax.numpy as jnp
from jax import lax
from jax.experimental import pallas as pl
from jax.experimental.pallas import tpu as pltpu
from jax.sharding import PartitionSpec as P

LANES = 128
ATTN_PIECES = 3
MLP_PIECES = 9
PIECES = ATTN_PIECES + MLP_PIECES
CHUNK = 96
WIDEN = 288
MESH = pl.DeviceIdType.MESH

D = 576
HEADS = 9
KV_HEADS = 3
HEAD_DIM = 64
FF = 1536
SEQ_LEN = 192


EPS = 1e-05
THETA = 100000.0


def mix(form, left, right):
    return jnp.einsum(form, left, right, preferred_element_type=jnp.float32)


def matmul(left, right):
    return jnp.dot(left, right, preferred_element_type=jnp.float32)


def inner(left, right):
    return lax.dot_general(
        left, right, (((0,), (0,)), ((), ())), preferred_element_type=jnp.float32
    )


def outer_t(left, right):
    return lax.dot_general(
        left, right, (((1,), (1,)), ((), ())), preferred_element_type=jnp.float32
    )


def split_attention(flat):
    kv_width = KV_HEADS * HEAD_DIM
    edge_one = D * D
    edge_two = edge_one + D * kv_width
    edge_three = edge_two + D * kv_width
    return (
        flat[:edge_one].reshape(D, D),
        flat[edge_one:edge_two].reshape(D, kv_width),
        flat[edge_two:edge_three].reshape(D, kv_width),
        flat[edge_three:].reshape(D, D),
    )


def split_mlp(flat):
    edge_one = D * FF
    return (
        flat[:edge_one].reshape(D, FF),
        flat[edge_one : 2 * edge_one].reshape(D, FF),
        flat[2 * edge_one :].reshape(FF, D),
    )


def rope_tables():
    position = jnp.arange(SEQ_LEN).astype(jnp.float32)
    frequency = THETA ** (-(jnp.arange(HEAD_DIM // 2).astype(jnp.float32) * 2.0 / HEAD_DIM))
    angles = position[:, None] * frequency[None, :]
    return (jnp.cos(angles), jnp.sin(angles))


def rotate(tensor, cosine, sine_tab):
    half_dim = tensor.shape[-1] // 2
    lower_half = tensor[..., :half_dim]
    upper_half = tensor[..., half_dim:]
    cos_wide = cosine[None, :, None, :]
    sin_wide = sine_tab[None, :, None, :]
    return jnp.concatenate(
        [
            lower_half * cos_wide - upper_half * sin_wide,
            upper_half * cos_wide + lower_half * sin_wide,
        ],
        axis=-1,
    )


def norm_forward(stream, gain_row):
    inv_rms = lax.rsqrt(jnp.mean(stream * stream, axis=-1, keepdims=True) + EPS)
    normed = stream * inv_rms
    return (normed, inv_rms, (normed * gain_row).astype(jnp.bfloat16))


def norm_backward(grad_in, normed, inv_rms, gain_row):
    scaled = grad_in * gain_row
    grad_stream = inv_rms * (scaled - normed * jnp.mean(scaled * normed, axis=-1, keepdims=True))
    return (grad_stream, jnp.sum(grad_in * normed, axis=0))


def scores_of(queries, key_rot):
    raw_scores = mix("sqkgd,stkd->skgqt", queries, key_rot) * HEAD_DIM ** (-0.5)
    causal = jnp.arange(SEQ_LEN)[:, None] >= jnp.arange(SEQ_LEN)[None, :]
    return jnp.where(causal, raw_scores, -jnp.inf)


def forward(stream, attn_weights, mlp_weights, gain_rows):
    w_query, w_key, w_value, w_out = attn_weights
    w_gate, w_up, w_down = mlp_weights
    row_count = stream.shape[0]
    seq_count = row_count // SEQ_LEN
    group_size = HEADS // KV_HEADS
    cosine, sine_tab = rope_tables()
    normed_one, inv_one, entry_one = norm_forward(stream, gain_rows[0])
    queries = matmul(entry_one, w_query).reshape(seq_count, SEQ_LEN, HEADS, HEAD_DIM)
    queries = (
        rotate(queries, cosine, sine_tab)
        .astype(jnp.bfloat16)
        .reshape(seq_count, SEQ_LEN, KV_HEADS, group_size, HEAD_DIM)
    )
    key_rot = rotate(
        matmul(entry_one, w_key).reshape(seq_count, SEQ_LEN, KV_HEADS, HEAD_DIM), cosine, sine_tab
    ).astype(jnp.bfloat16)
    values = (
        matmul(entry_one, w_value)
        .astype(jnp.bfloat16)
        .reshape(seq_count, SEQ_LEN, KV_HEADS, HEAD_DIM)
    )
    scores = scores_of(queries, key_rot)
    row_top = jnp.max(scores, axis=-1, keepdims=True)
    log_total = row_top + jnp.log(jnp.sum(jnp.exp(scores - row_top), axis=-1, keepdims=True))
    attn_probs = jnp.exp(scores - log_total).astype(jnp.bfloat16)
    context = (
        mix("skgqt,stkd->sqkgd", attn_probs, values).astype(jnp.bfloat16).reshape(row_count, D)
    )
    middle = stream + matmul(context, w_out)
    normed_two, inv_two, entry_two = norm_forward(middle, gain_rows[1])
    gate_pre = matmul(entry_two, w_gate)
    upward = matmul(entry_two, w_up)
    hidden = (jax.nn.silu(gate_pre) * upward).astype(jnp.bfloat16)
    output = middle + matmul(hidden, w_down)
    kept_state = (
        normed_one,
        inv_one,
        entry_one,
        queries,
        key_rot,
        values,
        log_total,
        context,
        normed_two,
        inv_two,
        entry_two,
        gate_pre,
        upward,
        hidden,
    )
    return (output, kept_state)


def mlp_backward(grad_out, kept_state, mlp_weights, gain_rows):
    normed_two, inv_two, entry_two, gate_pre, upward, hidden = kept_state[8:]
    w_gate, w_up, w_down = mlp_weights
    grad_bf = grad_out.astype(jnp.bfloat16)
    grad_down = inner(hidden, grad_bf)
    grad_hidden = outer_t(grad_bf, w_down)
    sigma = jax.nn.sigmoid(gate_pre)
    grad_gate = (grad_hidden * upward * sigma * (1.0 + gate_pre * (1.0 - sigma))).astype(
        jnp.bfloat16
    )
    grad_upward = (grad_hidden * gate_pre * sigma).astype(jnp.bfloat16)
    grad_gate_w = inner(entry_two, grad_gate)
    grad_up_w = inner(entry_two, grad_upward)
    grad_entry = outer_t(grad_gate, w_gate) + outer_t(grad_upward, w_up)
    grad_norm, gain_two = norm_backward(grad_entry, normed_two, inv_two, gain_rows[1])
    flat_grad = flatten([grad_gate_w, grad_up_w, grad_down])
    return (grad_out + grad_norm, flat_grad, gain_two)


def attn_backward(grad_middle, kept_state, attn_weights, gain_rows):
    normed_one, inv_one, entry_one, queries, key_rot, values, log_total, context = kept_state[:8]
    w_query, w_key, w_value, w_out = attn_weights
    row_count = grad_middle.shape[0]
    seq_count = row_count // SEQ_LEN
    group_size = HEADS // KV_HEADS
    kv_width = KV_HEADS * HEAD_DIM
    cosine, sine_tab = rope_tables()
    grad_bf = grad_middle.astype(jnp.bfloat16)
    grad_out_w = inner(context, grad_bf)
    grad_context = (
        outer_t(grad_bf, w_out)
        .astype(jnp.bfloat16)
        .reshape(seq_count, SEQ_LEN, KV_HEADS, group_size, HEAD_DIM)
    )
    soft_probs = jnp.exp(scores_of(queries, key_rot) - log_total)
    grad_soft = mix("sqkgd,stkd->skgqt", grad_context, values)
    row_dot = jnp.sum(soft_probs * grad_soft, axis=-1, keepdims=True)
    grad_scores = (soft_probs * (grad_soft - row_dot) * HEAD_DIM ** (-0.5)).astype(jnp.bfloat16)
    grad_query = mix("skgqt,stkd->sqkgd", grad_scores, key_rot).reshape(
        seq_count, SEQ_LEN, HEADS, HEAD_DIM
    )
    grad_query = rotate(grad_query, cosine, -sine_tab).astype(jnp.bfloat16).reshape(row_count, D)
    grad_key = (
        rotate(mix("skgqt,sqkgd->stkd", grad_scores, queries), cosine, -sine_tab)
        .astype(jnp.bfloat16)
        .reshape(row_count, kv_width)
    )
    grad_value = (
        mix("skgqt,sqkgd->stkd", soft_probs.astype(jnp.bfloat16), grad_context)
        .astype(jnp.bfloat16)
        .reshape(row_count, kv_width)
    )
    grad_entry = (
        outer_t(grad_query, w_query) + outer_t(grad_key, w_key) + outer_t(grad_value, w_value)
    )
    grad_norm, gain_one = norm_backward(grad_entry, normed_one, inv_one, gain_rows[0])
    flat_grad = flatten(
        [
            inner(entry_one, grad_query),
            inner(entry_one, grad_key),
            inner(entry_one, grad_value),
            grad_out_w,
        ]
    )
    return (grad_middle + grad_norm, flat_grad, gain_one)


def bit_count(devices):
    bits = devices.bit_length() - 1
    assert 1 << bits == devices
    return bits


def bit_orders(bits):
    upper = list(range(bits - 1, 2, -1))
    if bits < 3:
        return [list(range(bits - 1, -1, -1))] * PIECES
    late, early = upper + [2, 1, 0], upper + [1, 2, 0]
    one, two = [1] + upper + [2, 0], [2] + upper + [1, 0]
    cycle = (late, one, two, early, one, two)
    return [cycle[piece % len(cycle)] for piece in range(PIECES)]


GROUP = 3


def waves(bits):
    groups = PIECES // GROUP
    return [
        [
            (group * GROUP + member, step - group)
            for group in range(groups)
            if 0 <= step - group < bits
            for member in range(GROUP)
        ]
        for step in range(bits + groups - 1)
    ]


def coordinates(bits):
    me = lax.axis_index("dp")
    digits = [lax.rem(me // (1 << bit), 2) for bit in range(bits)]
    partners = [me + (1 << bit) * (1 - 2 * digits[bit]) for bit in range(bits)]
    return digits, partners


def meet(partners):
    barrier = pltpu.get_barrier_semaphore()
    for partner in partners:
        pl.semaphore_signal(barrier, inc=1, device_id=(partner,), device_id_type=MESH)
    pl.semaphore_wait(barrier, len(partners))


def pick(bits, fixed):
    return tuple(fixed.get(bit, slice(None)) for bit in range(bits - 1, -1, -1))


def locate(piece):
    return (0, piece // 4) if piece % 4 == 0 else (1, piece - piece // 4 - 1)


def gather_kernel(bits, attn_ref, mlp_ref, attn_full, mlp_full, local_sem, send_sem, recv_sem):
    digits, partners = coordinates(bits)
    orders = bit_orders(bits)
    fulls = (attn_full, mlp_full)
    here = pick(bits, dict(enumerate(digits)))
    own = [
        pltpu.make_async_copy(shard, full.at[here], local_sem.at[number])
        for number, (shard, full) in enumerate(zip((attn_ref, mlp_ref), fulls))
    ]
    for copy in own:
        copy.start()
    meet(partners)
    for copy in own:
        copy.wait()
    flights = {}
    for wave in waves(bits):
        for piece, stage in wave:
            if stage > 0:
                flights[piece, stage - 1].wait_recv()
            order = orders[piece]
            fixed = {bit: digits[bit] for bit in order[stage:]}
            array, spot = locate(piece)
            block = fulls[array].at[pick(bits, fixed) + (spot,)]
            copy = pltpu.make_async_remote_copy(
                src_ref=block,
                dst_ref=block,
                send_sem=send_sem.at[piece, stage],
                recv_sem=recv_sem.at[piece, stage],
                device_id=(partners[order[stage]],),
                device_id_type=MESH,
            )
            copy.start()
            flights[piece, stage] = copy
    for piece in range(PIECES):
        flights[piece, bits - 1].wait_recv()
    for copy in flights.values():
        copy.wait_send()


def gather(attn_shard, mlp_shard):
    devices = lax.axis_size("dp")
    bits = bit_count(devices)
    attn = attn_shard.reshape(ATTN_PIECES, -1, LANES)
    mlp = mlp_shard.reshape(MLP_PIECES, -1, LANES)
    vmem = pl.BlockSpec(memory_space=pltpu.VMEM)
    attn_full, mlp_full = pl.pallas_call(
        lambda *refs: gather_kernel(bits, *refs),
        out_shape=tuple(
            jax.ShapeDtypeStruct((2,) * bits + part.shape, part.dtype) for part in (attn, mlp)
        ),
        in_specs=[vmem, vmem],
        out_specs=(vmem, vmem),
        scratch_shapes=[
            pltpu.SemaphoreType.DMA((2,)),
            pltpu.SemaphoreType.DMA((PIECES, bits)),
            pltpu.SemaphoreType.DMA((PIECES, bits)),
        ],
        compiler_params=pltpu.CompilerParams(
            collective_id=0, has_side_effects=True, vmem_limit_bytes=16 << 20
        ),
    )(attn, mlp)
    return attn_full.reshape(-1, LANES), mlp_full.reshape(-1, LANES)


def strided(start, size, stride):
    return pl.ds(start, size, stride=stride)


def low_half(shape):
    return lax.broadcasted_iota(jnp.int32, shape, 1) < LANES // 2


def swap_halves(block):
    return pltpu.roll(block, LANES // 2, axis=1)


def unflatten_one(flat_ref, first_row, wide, pair, out_ref):
    rows, columns = out_ref.shape
    blocks, rest = divmod(columns, LANES)

    @pl.loop(0, rows * columns // LANES // WIDEN)
    def _(step):
        start = pl.multiple_of(step * WIDEN, WIDEN)
        wide[pl.ds(start, WIDEN), :] = flat_ref[pl.ds(first_row + start, WIDEN), :].astype(
            jnp.float32
        )

    @pl.loop(0, rows // CHUNK)
    def _(step):
        base = step * (CHUNK * columns // LANES)
        target = pl.ds(pl.multiple_of(step * CHUNK, CHUNK), CHUNK)
        if rest == 0:
            for block in range(blocks):
                out_ref[target, block * LANES : (block + 1) * LANES] = wide[
                    strided(base + block, CHUNK, blocks), :
                ].astype(jnp.bfloat16)
        else:
            period, half = 2 * blocks + 1, CHUNK // 2
            lines = [wide[strided(base + line, half, period), :] for line in range(period)]
            turned = [swap_halves(line) for line in lines[blocks:]]
            low = low_half((half, LANES))
            for block in range(blocks + 1):
                odd = turned[block]
                if block < blocks:
                    odd = jnp.where(low, odd, turned[block + 1])
                pair[block, strided(0, half, 2), :] = lines[block]
                pair[block, strided(1, half, 2), :] = odd
            for block in range(blocks):
                out_ref[target, block * LANES : (block + 1) * LANES] = pair[block].astype(
                    jnp.bfloat16
                )
            out_ref[target, blocks * LANES :] = pair[blocks][:, :rest].astype(jnp.bfloat16)


def flatten_one(grad_ref, first_row, wide, pair, flat_ref):
    rows, columns = grad_ref.shape
    blocks, rest = divmod(columns, LANES)

    @pl.loop(0, rows // CHUNK)
    def _(step):
        base = step * (CHUNK * columns // LANES)
        origin = pl.ds(pl.multiple_of(step * CHUNK, CHUNK), CHUNK)
        if rest == 0:
            for block in range(blocks):
                wide[strided(base + block, CHUNK, blocks), :] = grad_ref[
                    origin, block * LANES : (block + 1) * LANES
                ].astype(jnp.float32)
        else:
            period, half = 2 * blocks + 1, CHUNK // 2
            for block in range(blocks):
                pair[block] = grad_ref[origin, block * LANES : (block + 1) * LANES].astype(
                    jnp.float32
                )
            tail = grad_ref[origin, blocks * LANES :].astype(jnp.float32)
            pair[blocks] = jnp.concatenate([tail, tail], axis=1)
            even = [pair[block, strided(0, half, 2), :] for block in range(blocks + 1)]
            turned = [
                swap_halves(pair[block, strided(1, half, 2), :]) for block in range(blocks + 1)
            ]
            low = low_half((half, LANES))
            lines = even[:blocks] + [jnp.where(low, even[blocks], turned[0])]
            lines += [
                jnp.where(low, turned[block], turned[block + 1]) for block in range(blocks)
            ]
            for line in range(period):
                wide[strided(base + line, half, period), :] = lines[line]

    @pl.loop(0, rows * columns // LANES // WIDEN)
    def _(step):
        start = pl.multiple_of(step * WIDEN, WIDEN)
        flat_ref[pl.ds(first_row + start, WIDEN), :] = wide[pl.ds(start, WIDEN), :].astype(
            jnp.bfloat16
        )


KV_WIDTH = KV_HEADS * HEAD_DIM
ATTN_SHAPES = ((D, D), (D, KV_WIDTH), (D, KV_WIDTH), (D, D))
MLP_SHAPES = ((D, FF), (D, FF), (FF, D))


def relayout_scratch():
    longest = max(rows * columns for rows, columns in ATTN_SHAPES + MLP_SHAPES) // LANES
    widest = max(columns for _, columns in ATTN_SHAPES + MLP_SHAPES) // LANES + 1
    return [
        pltpu.VMEM((longest, LANES), jnp.float32),
        pltpu.VMEM((widest, CHUNK, LANES), jnp.float32),
    ]


def relayout(one, shapes, to_flat):
    def kernel(*refs):
        wide, pair = refs[-2:]
        flat_ref = refs[-3] if to_flat else refs[0]
        matrices = refs[:-3] if to_flat else refs[1:-2]
        first_row = 0
        for matrix in matrices:
            one(*((matrix, first_row, wide, pair, flat_ref) if to_flat else
                  (flat_ref, first_row, wide, pair, matrix)))
            first_row += matrix.shape[0] * matrix.shape[1] // LANES

    vmem = pl.BlockSpec(memory_space=pltpu.VMEM)
    total = sum(rows * columns for rows, columns in shapes) // LANES
    flat = jax.ShapeDtypeStruct((total, LANES), jnp.bfloat16)
    many = tuple(jax.ShapeDtypeStruct(shape, jnp.bfloat16) for shape in shapes)
    return pl.pallas_call(
        kernel,
        out_shape=flat if to_flat else many,
        in_specs=[vmem] * (len(shapes) if to_flat else 1),
        out_specs=vmem if to_flat else (vmem,) * len(shapes),
        scratch_shapes=relayout_scratch(),
        compiler_params=pltpu.CompilerParams(vmem_limit_bytes=20 << 20),
    )


def unflatten(flat, shapes):
    return relayout(unflatten_one, shapes, False)(flat)


def flatten(grads):
    shapes = tuple(grad.shape for grad in grads)
    return relayout(flatten_one, shapes, True)(*[grad.astype(jnp.bfloat16) for grad in grads])


def scatter_kernel(bits, attn_ref, mlp_ref, gain_ref, attn_out, mlp_out, gain_out, *scratch):
    totals = (attn_ref, mlp_ref)
    outs = (attn_out, mlp_out)
    landing = scratch[:bits]
    held = scratch[bits : 2 * bits - 1]
    gain_sent, gain_landing = scratch[2 * bits - 1 : 2 * bits + 1]
    send_sem, recv_sem, gain_send, gain_recv = scratch[2 * bits + 1 :]
    digits, partners = coordinates(bits)
    orders = [order[::-1] for order in bit_orders(bits)]
    meet(partners)
    flights = {}
    gain_flights = {}

    def block_index(order, stage, digit):
        if stage == 0:
            return pick(bits, {order[0]: digit})
        left = [bit for bit in range(bits - 1, -1, -1) if bit not in order[:stage]]
        return tuple(digit if bit == order[stage] else slice(None) for bit in left)

    def launch(piece, stage):
        order = orders[piece]
        bit = order[stage]
        lead = block_index(order, stage, 1 - digits[bit])
        if stage == 0:
            array, place = locate(piece)
            src = totals[array].at[lead + (place,)]
        else:
            src = held[stage - 1].at[(piece,) + lead]
        copy = pltpu.make_async_remote_copy(
            src_ref=src,
            dst_ref=landing[stage].at[piece],
            send_sem=send_sem.at[piece, stage],
            recv_sem=recv_sem.at[piece, stage],
            device_id=(partners[bit],),
            device_id_type=MESH,
        )
        copy.start()
        flights[piece, stage] = copy

    def absorb(piece, stage):
        flights[piece, stage].wait_recv()
        order = orders[piece]
        bit = order[stage]
        lead = block_index(order, stage, digits[bit])
        free = len(lead) - 1
        array, slot = locate(piece)
        for number in range(1 << free):
            picks = [(number >> place) & 1 for place in range(free - 1, -1, -1)]
            spot = iter(picks)
            where = tuple(next(spot) if isinstance(item, slice) else item for item in lead)
            if stage == 0:
                mine = totals[array][where + (slot,)]
            else:
                mine = held[stage - 1][(piece,) + where]
            other = landing[stage][(piece,) + tuple(picks)]
            value = mine.astype(jnp.float32) + other.astype(jnp.float32)
            if stage == bits - 1:
                outs[array][slot] = value
            else:
                held[stage][(piece,) + tuple(picks)] = value.astype(jnp.bfloat16)

    def launch_gain(stage):
        copy = pltpu.make_async_remote_copy(
            src_ref=gain_ref if stage == 0 else gain_sent.at[stage],
            dst_ref=gain_landing.at[stage],
            send_sem=gain_send.at[stage],
            recv_sem=gain_recv.at[stage],
            device_id=(partners[stage],),
            device_id_type=MESH,
        )
        copy.start()
        gain_flights[stage] = copy

    def absorb_gain(stage):
        gain_flights[stage].wait_recv()
        mine = gain_ref[...] if stage == 0 else gain_sent[stage]
        value = mine + gain_landing[stage]
        if stage == bits - 1:
            gain_out[...] = value
        else:
            gain_sent[stage + 1] = value

    for step, wave in enumerate(waves(bits)):
        if 0 < step < bits:
            absorb_gain(step - 1)
        if step < bits:
            launch_gain(step)
        for piece, stage in wave:
            if stage > 0:
                absorb(piece, stage - 1)
            launch(piece, stage)
    absorb_gain(bits - 1)
    for piece in range(PIECES):
        absorb(piece, bits - 1)
    for copy in list(flights.values()) + list(gain_flights.values()):
        copy.wait_send()


def scatter(attn_flat, mlp_flat, gains):
    devices = lax.axis_size("dp")
    bits = bit_count(devices)
    attn = attn_flat.reshape((2,) * bits + (ATTN_PIECES, -1, LANES))
    mlp = mlp_flat.reshape((2,) * bits + (MLP_PIECES, -1, LANES))
    rows = mlp.shape[-2]
    slots = [(PIECES,) + (2,) * (bits - 1 - stage) + (rows, LANES) for stage in range(bits)]
    vmem = pl.BlockSpec(memory_space=pltpu.VMEM)
    attn_sum, mlp_sum, gain_sum = pl.pallas_call(
        lambda *refs: scatter_kernel(bits, *refs),
        out_shape=(
            jax.ShapeDtypeStruct((ATTN_PIECES, rows, LANES), jnp.float32),
            jax.ShapeDtypeStruct((MLP_PIECES, rows, LANES), jnp.float32),
            jax.ShapeDtypeStruct(gains.shape, jnp.float32),
        ),
        in_specs=[vmem] * 3,
        out_specs=(vmem,) * 3,
        scratch_shapes=[pltpu.VMEM(slot, jnp.bfloat16) for slot in slots]
        + [pltpu.VMEM(slot, jnp.bfloat16) for slot in slots[:-1]]
        + [
            pltpu.VMEM((bits,) + gains.shape, jnp.float32),
            pltpu.VMEM((bits,) + gains.shape, jnp.float32),
            pltpu.SemaphoreType.DMA((PIECES, bits)),
            pltpu.SemaphoreType.DMA((PIECES, bits)),
            pltpu.SemaphoreType.DMA((bits,)),
            pltpu.SemaphoreType.DMA((bits,)),
        ],
        compiler_params=pltpu.CompilerParams(
            collective_id=1, has_side_effects=True, vmem_limit_bytes=32 << 20
        ),
    )(attn, mlp, gains)
    return attn_sum.reshape(-1), mlp_sum.reshape(-1), gain_sum


def body(inputs, cotangent, attn_shard, mlp_shard, gain_rows):
    attn_full, mlp_full = gather(attn_shard, mlp_shard)
    attn_weights = unflatten(attn_full, ATTN_SHAPES)
    mlp_weights = unflatten(mlp_full, MLP_SHAPES)
    outputs, kept_state = forward(inputs, attn_weights, mlp_weights, gain_rows)
    grad_middle, mlp_flat, gain_two = mlp_backward(cotangent, kept_state, mlp_weights, gain_rows)
    grad_input, attn_flat, gain_one = attn_backward(
        grad_middle, kept_state, attn_weights, gain_rows
    )
    gains = jnp.stack([gain_one, gain_two])
    attn_grad, mlp_grad, gain_grad = scatter(attn_flat, mlp_flat, gains)
    return (outputs, grad_input, attn_grad, mlp_grad, gain_grad)


def solution(mesh):
    placed = (P("dp", None), P("dp", None), P("dp"), P("dp"), P())
    return jax.shard_map(
        body,
        mesh=mesh,
        in_specs=placed,
        out_specs=(P("dp", None), P("dp", None), P("dp"), P("dp"), P()),
        check_vma=False,
    )
```
